32 devices in a mesh: rows: 8 (over z, y), modes: 4 (over x, core).
Axes of the slice: x: 2, y: 2, z: 4, core: 2. Of those that a mesh axis runs over, the one named last changes fastest.
Arguments:
- mode_slab: bfloat16 [4096, 512], P('rows', 'modes'), may hold values from -25 to 25
- mass_diag: float32 [4096], P('rows'), may hold values from 9.5 to 19
- mass_gain: float32 [4096], P('rows'), may hold values from 0.5 to 1.5
- band_coef: float32 [4], replicated, may hold values from 0.2 to 0.5
- band_offsets: int32 [4], replicated, may hold values from 1 to 64, as said below
- boundary_blocks: int32 [16, 4], P('rows'), may hold values from 0 to 31, as said below
- boundary_counts: int32 [16], P('rows'), may hold values from 2 to 4, as said below
- boundary_modes: bfloat16 [16, 512, 512], P('rows'), may hold values from -0.5 to 0.5
Outputs:
- projected: bfloat16 [16, 512, 512], P('rows', 'modes')
The draws below stay inside these ranges and needn't reach their ends.
Inputs may be any that keep to these rules, and one draw needn't show every extreme that they name: `band_offsets`: the offsets are distinct and one of them equals 64. `boundary_blocks`: entries of one component are distinct. For component c with e = c // 2, every entry b (used or not) satisfies (b - e * 4 + 512 // 256) mod (32) < 8. Among the used entries of the components of each index e of rows, one is the block just below e's rows and one the block just above them, counted cyclically. `boundary_counts`: some component uses all 4 blocks.
All inputs are finite; a program needn't handle non-finite values.
Results may differ from the reference program's by a relative error of at most 0.0035.
The reference program's roundings to bfloat16 on the way (of `scaled`, `mass_image`, `inverse` and `mass_basis`) count: a program that leaves them out, or rounds other values in their place, can miss the bound.
Values may be sent and summed in bfloat16 or wider, within the bound.
No kernel may reach another device: no remote copies, remote signals or barrier semaphores. Data moves between devices by JAX's collectives and lax.ppermute only.
A program may use at most 64 MiB of HBM per device.

```python
import math
import jax
import jax.numpy as jnp
from jax import lax

K = 512
CB = 512
BLOCK = 128
BMAX = 4
NOFF = 4
BAND = 64
ROWS_DEV = 512
COMP_DEV = 2
NDOF = 4096
NCOMP = 16


def draw_mode_slab(key, part):
    key_scale, key_base = jax.random.split(key, 2)
    scales = jnp.exp(jax.random.uniform(key_scale, (K,), jnp.float32, 0.0, math.log(10.0)))
    values = jnp.clip(jax.random.normal(key_base, (NDOF, K), jnp.float32), -7.0, 7.0)
    values = (values + 0.6 * jnp.roll(values, 1, axis=1)) / 1.6
    return jnp.clip(values * scales[None, :] / 3.0, -25.0, 25.0).astype(jnp.bfloat16)


def draw_band_offsets(key, part):
    shuffled = jax.random.permutation(key, BAND - 1)[:NOFF - 1] + 1
    chosen_values = jnp.concatenate([shuffled.astype(jnp.int32), jnp.full((1,), BAND, jnp.int32)])
    return jax.random.permutation(jax.random.fold_in(key, 1), chosen_values).astype(jnp.int32)


def boundary_layout(key):
    key = jax.random.fold_in(key, 7)
    key_rank, key_pick, key_offset, key_load, key_extra, key_force = jax.random.split(key, 6)
    row_devices = NCOMP // COMP_DEV
    dev_blocks = ROWS_DEV // BLOCK
    all_blocks = dev_blocks * row_devices
    half_blocks = dev_blocks // 2
    sub_window = 2 * dev_blocks // BMAX
    owner = jnp.arange(NCOMP, dtype=jnp.int32) // COMP_DEV
    position = jnp.arange(NCOMP, dtype=jnp.int32) % COMP_DEV
    chosen = jax.random.randint(key_pick, (row_devices,), 0, COMP_DEV).astype(jnp.int32)
    left_comp = position == chosen[owner]
    right_comp = position == (chosen[owner] + 1) % COMP_DEV
    slots = jnp.arange(BMAX, dtype=jnp.int32)
    scores = jax.random.randint(key_rank, (NCOMP, BMAX), 0, 1 << 20).astype(jnp.int32) * BMAX + slots[None, :]
    heavy = BMAX << 22
    scores = scores - jnp.where(left_comp[:, None] & (slots[None, :] == 0), 2 * heavy, 0)
    scores = scores - jnp.where(right_comp[:, None] & (slots[None, :] == BMAX - 1), heavy, 0)
    ranking = jnp.argsort(scores, axis=1, stable=True).astype(jnp.int32)
    offset = jax.random.randint(key_offset, (NCOMP, BMAX), 0, sub_window).astype(jnp.int32)
    relative = ranking * sub_window + offset
    relative = jnp.where(left_comp[:, None] & (ranking == 0), half_blocks - 1, relative)
    relative = jnp.where(right_comp[:, None] & (ranking == BMAX - 1), half_blocks + dev_blocks, relative)
    blocks = jnp.mod(owner[:, None] * dev_blocks - half_blocks + relative, all_blocks).astype(jnp.int32)
    device_load = jax.random.randint(key_load, (row_devices,), 1, BMAX).astype(jnp.int32)
    extra_blocks = jax.random.randint(key_extra, (NCOMP,), 0, device_load[owner] + 1).astype(jnp.int32)
    counts = jnp.minimum(BMAX, 2 + extra_blocks)
    forced = jax.random.randint(key_force, (), 0, NCOMP)
    counts = jnp.where(jnp.arange(NCOMP, dtype=jnp.int32) == forced, BMAX, counts).astype(jnp.int32)
    return (blocks, counts)


def draw_boundary_blocks(key, part):
    return boundary_layout(key)[0]


def draw_boundary_counts(key, part):
    return boundary_layout(key)[1]


def block_scale(stream_key, dims, pieces, smallest, top_value):
    gain, own = 1.0, jax.random.fold_in(stream_key, 6)
    for axis_at, parts in pieces:
        draws = jnp.exp(jax.random.uniform(jax.random.fold_in(own, axis_at), (parts,), jnp.float32, smallest / len(pieces), top_value / len(pieces)))
        gain = gain * jnp.repeat(draws, dims[axis_at] // parts).reshape([-1 if axis == axis_at else 1 for axis in range(len(dims))])
    return gain


def noise(rng, dims, scale, reach, shards=(), kind=jnp.bfloat16):
    drawn = jax.random.normal(rng, dims, jnp.float32) * scale
    if len(shards) > 0:
        drawn = block_scale(rng, dims, shards, -0.22, 0.18) * drawn
    return jnp.clip(drawn, min=-reach, max=reach).astype(kind)


def setup_inputs(seed: int = 0) -> dict:
    key_of = jax.random.split(jax.random.key(seed), 9)
    mode_slab = draw_mode_slab(jax.random.fold_in(key_of[8], 71), 0)
    mass_diag = jnp.clip(9.5 + 9.5 * jax.random.uniform(key_of[1], (NDOF,), jnp.float32) ** block_scale(key_of[1], (NDOF,), ((0, 8),), -0.2, 0.2), 9.5, 19.0)
    mass_gain = jnp.clip(1.0 + 0.1 * jax.random.normal(key_of[2], (NDOF,), jnp.float32), 0.5, 1.5)
    band_coef = jnp.clip(jax.random.uniform(key_of[3], (NOFF,), jnp.float32, 0.2, 0.5), 0.2, 0.5)
    band_offsets = draw_band_offsets(jax.random.fold_in(key_of[8], 71), 0)
    boundary_blocks = draw_boundary_blocks(jax.random.fold_in(key_of[8], 71), 0)
    boundary_counts = draw_boundary_counts(jax.random.fold_in(key_of[8], 71), 0)
    boundary_modes = noise(key_of[7], (NCOMP, BMAX * BLOCK, CB), BLOCK ** -0.5, 0.5, ((0, 8),))
    return dict(mode_slab=mode_slab, mass_diag=mass_diag, mass_gain=mass_gain, band_coef=band_coef, band_offsets=band_offsets, boundary_blocks=boundary_blocks, boundary_counts=boundary_counts, boundary_modes=boundary_modes)


def reference(mode_slab, mass_diag, mass_gain, band_coef, band_offsets, boundary_blocks, boundary_counts, boundary_modes):
    scaled = (mass_gain[:, None] * mode_slab.astype(jnp.float32)).astype(jnp.bfloat16)
    padded = jnp.pad(scaled, ((BAND, BAND), (0, 0)))
    neighbour = jnp.zeros(mode_slab.shape, jnp.float32)
    for j in range(NOFF):
        offset = band_offsets[j].astype(jnp.int32)
        upward = lax.dynamic_slice_in_dim(padded, BAND + offset, NDOF, 0)
        downward = lax.dynamic_slice_in_dim(padded, BAND - offset, NDOF, 0)
        neighbour = neighbour + band_coef[j] * (upward.astype(jnp.float32) + downward.astype(jnp.float32))
    mass_image = (mass_diag[:, None] * mode_slab.astype(jnp.float32) + mass_gain[:, None] * neighbour).astype(jnp.bfloat16)
    gram_matrix = jnp.dot(mass_image.T.astype(jnp.float32), mode_slab.astype(jnp.float32), preferred_element_type=jnp.float32) / NDOF
    lower_factor = jnp.linalg.cholesky(gram_matrix)
    identity = jnp.eye(K, dtype=jnp.float32)
    inverse = jax.scipy.linalg.solve_triangular(lower_factor, identity, lower=True, trans=1).astype(jnp.bfloat16)
    mass_basis = jnp.dot(mass_image.astype(jnp.float32), inverse.astype(jnp.float32), preferred_element_type=jnp.float32).astype(jnp.bfloat16)

    def project(entry):
        blocks, used_count, shapes_in = entry
        slot_rows = (blocks.astype(jnp.int32)[:, None] * BLOCK + jnp.arange(BLOCK, dtype=jnp.int32)[None, :]).reshape(-1)
        picked = jnp.take(mass_basis, slot_rows, axis=0)
        in_use = jnp.repeat(jnp.arange(BMAX, dtype=jnp.int32) < used_count, BLOCK)
        picked = jnp.where(in_use[:, None], picked, jnp.zeros_like(picked))
        return jnp.dot(picked.T.astype(jnp.float32), shapes_in.astype(jnp.float32), preferred_element_type=jnp.float32).astype(jnp.bfloat16)
    return lax.map(project, (boundary_blocks, boundary_counts, boundary_modes))
```

```python
import jax
import jax.numpy as jnp
from jax import lax
from jax.experimental import pallas as pl
from jax.experimental.pallas import tpu as pltpu
from jax.sharding import PartitionSpec as P

BLOCK = 128
BMAX = 4
NOFF = 4
BAND = 64

f32 = jnp.float32
bf16 = jnp.bfloat16
VMEM = pl.BlockSpec(memory_space=pltpu.VMEM)
SMEM = pl.BlockSpec(memory_space=pltpu.SMEM)


def halves(x):
    top = x.astype(bf16)
    rest = x - top.astype(f32)
    middle = rest.astype(bf16)
    return top, middle, (rest - middle.astype(f32)).astype(bf16)


def dot(a, b, dims=((1,), (0,))):
    return lax.dot_general(a, b, (dims, ((), ())), preferred_element_type=f32)


def dot_f32(a, b, dims=((1,), (0,))):
    return lax.dot_general(
        a, b, (dims, ((), ())), precision=lax.Precision.HIGHEST, preferred_element_type=f32
    )


def image_kernel(scale, where_ref, coef_ref, offset_ref, gathered, diag_ref, gain_ref, image, share, scaled, blocks):
    modes = gathered.shape[0]
    rows = diag_ref.shape[0]
    size = BLOCK
    wide = size + 2 * BAND
    row = lax.broadcasted_iota(jnp.int32, (size, wide), 0)
    column = lax.broadcasted_iota(jnp.int32, (size, wide), 1)
    distance = jnp.abs(column - row - BAND)
    band = jnp.zeros((size, wide), f32)
    for j in range(NOFF):
        band = band + jnp.where(distance == offset_ref[j], coef_ref[j], 0.0)
    parts = halves(band)
    for m in range(modes):
        lanes = slice(m * size, (m + 1) * size)
        scaled[0:BAND, lanes] = gathered[m, 0:BAND, :]
        scaled[BAND + rows :, lanes] = gathered[m, BAND + rows :, :]
        slab = gathered[m, BAND : BAND + rows, :].astype(f32)
        scaled[BAND : BAND + rows, lanes] = (gain_ref[...] * slab).astype(bf16)
    for i in range(rows // size):
        rows_in = scaled[i * size : i * size + wide, :]
        neighbour = dot(parts[0], rows_in) + dot(parts[1], rows_in) + dot(parts[2], rows_in)
        here = slice(i * size, (i + 1) * size)
        for m in range(modes):
            lanes = slice(m * size, (m + 1) * size)
            slab = gathered[m, BAND + i * size : BAND + (i + 1) * size, :].astype(f32)
            image[here, lanes] = (
                diag_ref[here, :] * slab + gain_ref[here, :] * neighbour[:, lanes]
            ).astype(bf16)
    for s in range(blocks.shape[0] // size):
        i, j = where_ref[2 * s], where_ref[2 * s + 1]
        image_i = image[:, pl.ds(pl.multiple_of(i * size, size), size)]
        image_j = image[:, pl.ds(pl.multiple_of(j * size, size), size)]
        slab_i = gathered[i, BAND : BAND + rows, :]
        slab_j = gathered[j, BAND : BAND + rows, :]
        over_rows = ((0,), (0,))
        blocks[s * size : (s + 1) * size, :] = (
            dot(image_i, slab_j, over_rows) + dot(slab_i, image_j, over_rows)
        ) * scale
    start = where_ref[2 * (blocks.shape[0] // size)]
    share[...] = blocks[pl.ds(pl.multiple_of(start, 8), share.shape[0]), :]


def lanes_of(x, t):
    return jnp.broadcast_to(x[:, t : t + 1], (8, BLOCK))


def rows_of(x, t):
    return jnp.broadcast_to(x[t : t + 1, :], (8, BLOCK))


def inverse_factor(square):
    panels = BLOCK // 8
    sub = lax.broadcasted_iota(jnp.int32, (8, BLOCK), 0)
    lane = lax.broadcasted_iota(jnp.int32, (8, BLOCK), 1)
    left = [square[8 * p : 8 * p + 8, :] for p in range(panels)]
    right = [(lane == sub + 8 * p).astype(f32) for p in range(panels)]
    result = []
    for p in range(panels):
        has_next = p + 1 < panels
        a, b = left[p], right[p]
        own = [lanes_of(a, 8 * p + t) for t in range(8)]
        if has_next:
            c, d = left[p + 1], right[p + 1]
            below = [lanes_of(c, 8 * p + t) for t in range(8)]
        pivots = jnp.ones((8, BLOCK), f32)
        inverses = jnp.ones((8, BLOCK), f32)
        for t in range(8):
            pivot = rows_of(own[t], t)
            inverse = 1.0 / pivot
            pivots = jnp.where(sub == t, pivot, pivots)
            inverses = jnp.where(sub == t, inverse, inverses)
            a_row, b_row = rows_of(a, t), rows_of(b, t)
            if has_next:
                g = below[t] * inverse
            if t < 7:
                f = jnp.where(sub > t, own[t] * inverse, 0.0)
                for u in range(t + 1, 8):
                    u_row = rows_of(own[u], t)
                    own[u] = own[u] - f * u_row
                    if has_next:
                        below[u] = below[u] - g * u_row
                a = a - f * a_row
                b = b - f * b_row
            if has_next:
                c = c - g * a_row
                d = d - g * b_row
        result.append(b * lax.rsqrt(pivots))
        if has_next:
            left[p + 1], right[p + 1] = c, d
        if p + 2 < panels:
            across = jnp.transpose(a * inverses)
            a_rows = [rows_of(a, t) for t in range(8)]
            b_rows = [rows_of(b, t) for t in range(8)]
            for i in range(p + 2, panels):
                factors = across[8 * i : 8 * i + 8, :]
                for t in range(8):
                    f = lanes_of(factors, t)
                    left[i] = left[i] - f * a_rows[t]
                    right[i] = right[i] - f * b_rows[t]
    return jnp.concatenate(result, axis=0)


def factor_kernel(which_ref, gram, inverse, schur, solved):
    count = inverse.shape[1] // BLOCK
    size = BLOCK
    place = lambda i, j: (i * (i + 1) // 2 + j) * size
    across = ((1,), (1,))
    schur[...] = gram[...]
    solved[...] = jnp.zeros(solved.shape, f32)
    for k in range(count):
        w = inverse_factor(schur[place(k, k) : place(k, k) + size, :])
        here = slice(k * size, (k + 1) * size)
        if k:
            solved[here, : k * size] = -dot_f32(w, solved[here, : k * size])
        solved[here, here] = w
        lower = [None] * count
        for i in range(k + 1, count):
            lower[i] = dot_f32(schur[place(i, k) : place(i, k) + size, :], w, across)
        for i in range(k + 1, count):
            for j in range(k + 1, i + 1):
                at = slice(place(i, j), place(i, j) + size)
                schur[at, :] = schur[at, :] - dot_f32(lower[i], lower[j], across)
        for i in range(k + 1, count):
            there = slice(i * size, (i + 1) * size)
            done = (k + 1) * size
            solved[there, :done] = solved[there, :done] + dot_f32(lower[i], solved[here, :done])
    mine = pl.multiple_of(which_ref[0] * size, size)
    inverse[...] = solved[pl.ds(mine, size), :].astype(bf16)


def project_kernel(blocks_ref, counts_ref, low, own, high, inverse, shapes, out, basis, picked):
    size = BLOCK
    across = ((1,), (1,))
    at = 0
    for part in (low, own, high):
        for i in range(part.shape[0] // size):
            rows = part[i * size : (i + 1) * size, :]
            basis[at] = dot(rows, inverse[...], across).astype(bf16)
            at += 1
    for c in range(out.shape[0]):
        for s in range(BMAX):
            rows = basis[blocks_ref[BMAX * c + s]]
            picked[s * size : (s + 1) * size, :] = jnp.where(s < counts_ref[c], rows, jnp.zeros_like(rows))
        out[c] = dot(picked[...], shapes[c], ((0,), (0,))).astype(bf16)


def sum_over_rows(value):
    count = lax.axis_size("rows")
    if count & (count - 1):
        return lax.psum(value, "rows")
    step = 1
    while step < count:
        value = value + lax.ppermute(value, "rows", [(i, i ^ step) for i in range(count)])
        step *= 2
    return value


def local(
    mode_slab,
    mass_diag,
    mass_gain,
    band_coef,
    band_offsets,
    boundary_blocks,
    boundary_counts,
    boundary_modes,
):
    rows_dev, mode_cols = mode_slab.shape
    modes = lax.axis_size("modes")
    row_devices = lax.axis_size("rows")
    order = mode_cols * modes
    count = order // BLOCK
    per_dev = rows_dev // BLOCK
    rim_rows = per_dev // 2 * BLOCK
    total_rows = rows_dev * row_devices
    up = [(i, i + 1) for i in range(row_devices - 1)]
    down = [(i + 1, i) for i in range(row_devices - 1)]

    def scaled_edge(rows):
        return (mass_gain[rows, None] * mode_slab[rows, :].astype(f32)).astype(bf16)

    low = lax.ppermute(scaled_edge(slice(rows_dev - BAND, rows_dev)), "rows", up)
    high = lax.ppermute(scaled_edge(slice(0, BAND)), "rows", down)
    gathered = lax.all_gather(jnp.concatenate([low, mode_slab, high], axis=0), "modes", axis=0)

    lower = [(i, j) for i in range(count) for j in range(i + 1)]
    share_rows = len(lower) * BLOCK // modes
    taken = -(-(share_rows + BLOCK // 2) // BLOCK)
    table = []
    for m in range(modes):
        first = m * share_rows // BLOCK
        first = min(first, len(lower) - taken)
        entries = [v for s in range(taken) for v in lower[first + s]]
        table.append(entries + [m * share_rows - first * BLOCK])
    mode_index = lax.axis_index("modes")
    where = jnp.asarray(table, jnp.int32)[mode_index]

    image, share = pl.pallas_call(
        lambda *refs: image_kernel(0.5 / total_rows, *refs),
        out_shape=(
            jax.ShapeDtypeStruct((rows_dev, order), bf16),
            jax.ShapeDtypeStruct((share_rows, BLOCK), f32),
        ),
        in_specs=[SMEM, SMEM, SMEM, VMEM, VMEM, VMEM],
        out_specs=(VMEM, VMEM),
        scratch_shapes=[
            pltpu.VMEM((rows_dev + 2 * BAND, order), bf16),
            pltpu.VMEM((taken * BLOCK, BLOCK), f32),
        ],
        name="image",
    )(where, band_coef, band_offsets, gathered, mass_diag[:, None], mass_gain[:, None])

    share = sum_over_rows(share)
    image, share = lax.optimization_barrier((image, share))
    around = [(i, (i + 1) % row_devices) for i in range(row_devices)]
    back = [(target, source) for source, target in around]
    rim_low = lax.ppermute(image[rows_dev - rim_rows :, :], "rows", around)
    rim_high = lax.ppermute(image[:rim_rows, :], "rows", back)
    gram = lax.all_gather(share, "modes", axis=0).reshape(len(lower) * BLOCK, BLOCK)

    inverse = pl.pallas_call(
        factor_kernel,
        out_shape=jax.ShapeDtypeStruct((BLOCK, order), bf16),
        in_specs=[SMEM, VMEM],
        out_specs=VMEM,
        scratch_shapes=[
            pltpu.VMEM((len(lower) * BLOCK, BLOCK), f32),
            pltpu.VMEM((order, order), f32),
        ],
        name="factor",
    )(mode_index.reshape(1).astype(jnp.int32), gram)

    total_blocks = per_dev * row_devices
    window_start = lax.axis_index("rows") * per_dev - per_dev // 2
    local_blocks = jnp.mod(boundary_blocks - window_start, total_blocks).reshape(-1)
    owned, _, width = boundary_modes.shape
    window = per_dev + 2 * (per_dev // 2)
    return pl.pallas_call(
        project_kernel,
        out_shape=jax.ShapeDtypeStruct((owned, mode_cols, width), bf16),
        in_specs=[SMEM, SMEM, VMEM, VMEM, VMEM, VMEM, VMEM],
        out_specs=VMEM,
        scratch_shapes=[
            pltpu.VMEM((window, BLOCK, BLOCK), bf16),
            pltpu.VMEM((BMAX * BLOCK, BLOCK), bf16),
        ],
        name="project",
    )(local_blocks, boundary_counts, rim_low, image, rim_high, inverse, boundary_modes)


def solution(mesh):
    in_specs = (
        P("rows", "modes"),
        P("rows"),
        P("rows"),
        P(),
        P(),
        P("rows", None),
        P("rows"),
        P("rows", None, None),
    )
    out_specs = P("rows", "modes", None)
    return jax.shard_map(local, mesh=mesh, in_specs=in_specs, out_specs=out_specs, check_vma=False)
```

```python
import jax
import jax.numpy as jnp
from jax import lax
from jax.experimental import pallas as pl
from jax.experimental.pallas import tpu as pltpu
from jax.sharding import PartitionSpec as P

BLOCK = 128
BMAX = 4
NOFF = 4
BAND = 64

f32 = jnp.float32
bf16 = jnp.bfloat16
VMEM = pl.BlockSpec(memory_space=pltpu.VMEM)


def near(x):
    return pltpu.with_memory_space_constraint(x, pltpu.VMEM)

SMEM = pl.BlockSpec(memory_space=pltpu.SMEM)


def bf16_parts(x):
    top = x.astype(bf16)
    rest = x - top.astype(f32)
    middle = rest.astype(bf16)
    return top, middle, (rest - middle.astype(f32)).astype(bf16)


def dot(a, b, dims=((1,), (0,))):
    return lax.dot_general(a, b, (dims, ((), ())), preferred_element_type=f32)


def dot_f32(a, b, dims=((1,), (0,))):
    return lax.dot_general(
        a, b, (dims, ((), ())), precision=lax.Precision.HIGHEST, preferred_element_type=f32
    )


def image_kernel(scale, where_ref, coef_ref, offset_ref, gathered, diag_ref, gain_ref, first, second, share, scaled, blocks):
    modes = gathered.shape[0]
    rows = diag_ref.shape[0]
    half = first.shape[0]
    size = BLOCK
    wide = size + 2 * BAND
    row = lax.broadcasted_iota(jnp.int32, (size, wide), 0)
    column = lax.broadcasted_iota(jnp.int32, (size, wide), 1)
    distance = jnp.abs(column - row - BAND)
    band = jnp.zeros((size, wide), f32)
    for j in range(NOFF):
        band = band + jnp.where(distance == offset_ref[j], coef_ref[j], 0.0)
    parts = bf16_parts(band)
    for m in range(modes):
        lanes = slice(m * size, (m + 1) * size)
        scaled[0:BAND, lanes] = gathered[m, 0:BAND, :]
        scaled[BAND + rows :, lanes] = gathered[m, BAND + rows :, :]
        slab = gathered[m, BAND : BAND + rows, :].astype(f32)
        scaled[BAND : BAND + rows, lanes] = (gain_ref[...] * slab).astype(bf16)
    for i in range(rows // size):
        rows_in = scaled[i * size : i * size + wide, :]
        neighbour = dot(parts[0], rows_in) + dot(parts[1], rows_in) + dot(parts[2], rows_in)
        here = slice(i * size, (i + 1) * size)
        for m in range(modes):
            lanes = slice(m * size, (m + 1) * size)
            slab = gathered[m, BAND + i * size : BAND + (i + 1) * size, :].astype(f32)
            image, at = (first, i * size) if i * size < half else (second, i * size - half)
            image[at : at + size, lanes] = (
                diag_ref[here, :] * slab + gain_ref[here, :] * neighbour[:, lanes]
            ).astype(bf16)
    for s in range(blocks.shape[0] // size):
        i, j = where_ref[2 * s], where_ref[2 * s + 1]
        total = jnp.zeros((size, size), f32)
        for image, at in ((first, BAND), (second, BAND + half)):
            image_i = image[:, pl.ds(pl.multiple_of(i * size, size), size)]
            image_j = image[:, pl.ds(pl.multiple_of(j * size, size), size)]
            slab_i = gathered[i, at : at + half, :]
            slab_j = gathered[j, at : at + half, :]
            over_rows = ((0,), (0,))
            total = total + dot(image_i, slab_j, over_rows) + dot(slab_i, image_j, over_rows)
        blocks[s * size : (s + 1) * size, :] = total * scale
    start = where_ref[2 * (blocks.shape[0] // size)]
    share[...] = blocks[pl.ds(pl.multiple_of(start, 8), share.shape[0]), :]


def lanes_of(x, t):
    return jnp.broadcast_to(x[:, t : t + 1], (8, BLOCK))


def rows_of(x, t):
    return jnp.broadcast_to(x[t : t + 1, :], (8, BLOCK))


def inverse_factor(square, depth=3):
    panels = BLOCK // 8
    sub = lax.broadcasted_iota(jnp.int32, (8, BLOCK), 0)
    lane = lax.broadcasted_iota(jnp.int32, (8, BLOCK), 1)
    left = [square[8 * p : 8 * p + 8, :] for p in range(panels)]
    right = [(lane == sub + 8 * p).astype(f32) for p in range(panels)]
    own = [lanes_of(left[0], t) for t in range(8)]
    result = []
    for p in range(panels):
        below = range(p + 1, min(panels, p + 1 + depth))
        columns = 16 if p + 1 < panels else 8
        a, b = left[p], right[p]
        own = own + [lanes_of(a, 8 * p + t) for t in range(8, columns)]
        under = {
            i: [lanes_of(left[i], 8 * p + t) for t in range(columns if i == p + 1 else 8)] for i in below
        }
        pivots = jnp.ones((8, BLOCK), f32)
        inverses = jnp.ones((8, BLOCK), f32)
        for t in range(8):
            pivot = rows_of(own[t], t)
            inverse = 1.0 / pivot
            pivots = jnp.where(sub == t, pivot, pivots)
            inverses = jnp.where(sub == t, inverse, inverses)
            f = jnp.where(sub > t, own[t], 0.0) * inverse
            g = {i: under[i][t] * inverse for i in below}
            for u in range(t + 1, columns):
                u_row = rows_of(own[u], t)
                if t < 7:
                    own[u] = own[u] - f * u_row
                for i in below:
                    if u < len(under[i]):
                        under[i][u] = under[i][u] - g[i] * u_row
            a_row, b_row = rows_of(a, t), rows_of(b, t)
            if t < 7:
                a = a - f * a_row
                b = b - f * b_row
            for i in below:
                left[i] = left[i] - g[i] * a_row
                right[i] = right[i] - g[i] * b_row
        result.append(b * lax.rsqrt(pivots))
        if p + 1 < panels:
            own = under[p + 1][8:]
        rest = p + 1 + depth
        if rest < panels:
            a0, a1, a2 = bf16_parts(a * inverses)
            b0, b1, b2 = bf16_parts(jnp.concatenate([a, b], axis=1))
            update = dot(
                jnp.concatenate([a0, a0, a1, a0, a2, a1], axis=0)[:, 8 * rest :],
                jnp.concatenate([b0, b1, b0, b2, b0, b1], axis=0),
                ((0,), (0,)),
            )
            for i in range(rest, panels):
                at = slice(8 * (i - rest), 8 * (i - rest) + 8)
                left[i] = left[i] - update[at, :BLOCK]
                right[i] = right[i] - update[at, BLOCK:]
    return jnp.concatenate(result, axis=0)


def factor_kernel(which_ref, gram, inverse, schur, solved):
    count = inverse.shape[1] // BLOCK
    size = BLOCK
    place = lambda i, j: (i * (i + 1) // 2 + j) * size
    across = ((1,), (1,))
    schur[...] = gram[...]
    solved[...] = jnp.zeros(solved.shape, f32)
    for k in range(count):
        w = inverse_factor(schur[place(k, k) : place(k, k) + size, :])
        here = slice(k * size, (k + 1) * size)
        if k:
            solved[here, : k * size] = -dot_f32(w, solved[here, : k * size])
        solved[here, here] = w
        lower = [None] * count
        for i in range(k + 1, count):
            lower[i] = dot_f32(schur[place(i, k) : place(i, k) + size, :], w, across)
        for i in range(k + 1, count):
            for j in range(k + 1, i + 1):
                at = slice(place(i, j), place(i, j) + size)
                schur[at, :] = schur[at, :] - dot_f32(lower[i], lower[j], across)
        for i in range(k + 1, count):
            there = slice(i * size, (i + 1) * size)
            done = (k + 1) * size
            solved[there, :done] = solved[there, :done] + dot_f32(lower[i], solved[here, :done])
    mine = pl.multiple_of(which_ref[0] * size, size)
    inverse[...] = solved[pl.ds(mine, size), :].astype(bf16)


def project_kernel(blocks_ref, counts_ref, low, first, second, high, inverse, shapes, out, basis, picked):
    size = BLOCK
    across = ((1,), (1,))
    at = 0
    for part in (low, first, second, high):
        for i in range(part.shape[0] // size):
            rows = part[i * size : (i + 1) * size, :]
            basis[at] = dot(rows, inverse[...], across).astype(bf16)
            at += 1
    for c in range(out.shape[0]):
        for s in range(BMAX):
            rows = basis[blocks_ref[BMAX * c + s]]
            picked[s * size : (s + 1) * size, :] = jnp.where(s < counts_ref[c], rows, jnp.zeros_like(rows))
        out[c] = dot(picked[...], shapes[c], ((0,), (0,))).astype(bf16)


def sum_over_rows(value):
    count = lax.axis_size("rows")
    if count & (count - 1):
        return lax.psum(value, "rows")
    step = 1
    while step < count:
        value = value + lax.ppermute(value, "rows", [(i, i ^ step) for i in range(count)])
        step *= 2
    return value


def local(
    mode_slab,
    mass_diag,
    mass_gain,
    band_coef,
    band_offsets,
    boundary_blocks,
    boundary_counts,
    boundary_modes,
):
    rows_dev, mode_cols = mode_slab.shape
    modes = lax.axis_size("modes")
    row_devices = lax.axis_size("rows")
    order = mode_cols * modes
    count = order // BLOCK
    per_dev = rows_dev // BLOCK
    rim_rows = per_dev // 2 * BLOCK
    total_rows = rows_dev * row_devices
    assert rows_dev == 2 * rim_rows
    up = [(i, i + 1) for i in range(row_devices - 1)]
    down = [(i + 1, i) for i in range(row_devices - 1)]

    def scaled_edge(rows):
        return (mass_gain[rows, None] * mode_slab[rows, :].astype(f32)).astype(bf16)

    low = lax.ppermute(scaled_edge(slice(rows_dev - BAND, rows_dev)), "rows", up)
    high = lax.ppermute(scaled_edge(slice(0, BAND)), "rows", down)
    gathered = lax.all_gather(jnp.concatenate([low, mode_slab, high], axis=0), "modes", axis=0)

    lower = [(i, j) for i in range(count) for j in range(i + 1)]
    share_rows = len(lower) * BLOCK // modes
    taken = -(-(share_rows + BLOCK // 2) // BLOCK)
    table = []
    for m in range(modes):
        first = m * share_rows // BLOCK
        first = min(first, len(lower) - taken)
        entries = [v for s in range(taken) for v in lower[first + s]]
        table.append(entries + [m * share_rows - first * BLOCK])
    mode_index = lax.axis_index("modes")
    where = jnp.asarray(table, jnp.int32)[mode_index]

    first, second, share = pl.pallas_call(
        lambda *refs: image_kernel(0.5 / total_rows, *refs),
        out_shape=(
            pltpu.VMEM((rim_rows, order), bf16),
            pltpu.VMEM((rim_rows, order), bf16),
            pltpu.VMEM((share_rows, BLOCK), f32),
        ),
        in_specs=[SMEM, SMEM, SMEM, VMEM, VMEM, VMEM],
        out_specs=(VMEM, VMEM, VMEM),
        scratch_shapes=[
            pltpu.VMEM((rows_dev + 2 * BAND, order), bf16),
            pltpu.VMEM((taken * BLOCK, BLOCK), f32),
        ],
        name="image",
    )(where, band_coef, band_offsets, near(gathered), near(mass_diag[:, None]), near(mass_gain[:, None]))

    share = sum_over_rows(share)
    first, second, share = lax.optimization_barrier((first, second, share))
    around = [(i, (i + 1) % row_devices) for i in range(row_devices)]
    back = [(target, source) for source, target in around]
    rim_low = lax.ppermute(second, "rows", around)
    rim_high = lax.ppermute(first, "rows", back)
    gram = lax.all_gather(share, "modes", axis=0).reshape(len(lower) * BLOCK, BLOCK)

    inverse = pl.pallas_call(
        factor_kernel,
        out_shape=pltpu.VMEM((BLOCK, order), bf16),
        in_specs=[SMEM, VMEM],
        out_specs=VMEM,
        scratch_shapes=[
            pltpu.VMEM((len(lower) * BLOCK, BLOCK), f32),
            pltpu.VMEM((order, order), f32),
        ],
        name="factor",
    )(mode_index.reshape(1).astype(jnp.int32), near(gram))

    total_blocks = per_dev * row_devices
    window_start = lax.axis_index("rows") * per_dev - per_dev // 2
    local_blocks = jnp.mod(boundary_blocks - window_start, total_blocks).reshape(-1)
    owned, _, width = boundary_modes.shape
    window = per_dev + 2 * (per_dev // 2)
    return pl.pallas_call(
        project_kernel,
        out_shape=jax.ShapeDtypeStruct((owned, mode_cols, width), bf16),
        in_specs=[SMEM, SMEM, VMEM, VMEM, VMEM, VMEM, VMEM, VMEM],
        out_specs=VMEM,
        scratch_shapes=[
            pltpu.VMEM((window, BLOCK, BLOCK), bf16),
            pltpu.VMEM((BMAX * BLOCK, BLOCK), bf16),
        ],
        name="project",
    )(local_blocks, boundary_counts, near(rim_low), near(first), near(second), near(rim_high), near(inverse), near(boundary_modes))


def solution(mesh):
    in_specs = (
        P("rows", "modes"),
        P("rows"),
        P("rows"),
        P(),
        P(),
        P("rows", None),
        P("rows"),
        P("rows", None, None),
    )
    out_specs = P("rows", "modes", None)
    return jax.shard_map(local, mesh=mesh, in_specs=in_specs, out_specs=out_specs, check_vma=False)
```

```python
import jax
import jax.numpy as jnp
from jax import lax
from jax.experimental import pallas as pl
from jax.experimental.pallas import tpu as pltpu
from jax.sharding import PartitionSpec as P

BLOCK = 128
BMAX = 4
NOFF = 4
BAND = 64
SHARES = (
    ((0, 0), (1, 1), (1, 0)),
    ((2, 2), (3, 3), (2, 0)),
    ((2, 1), (2, 1), (3, 0)),
    ((3, 1), (3, 1), (3, 2)),
)

f32 = jnp.float32
bf16 = jnp.bfloat16
VMEM = pl.BlockSpec(memory_space=pltpu.VMEM)


def near(x):
    return pltpu.with_memory_space_constraint(x, pltpu.VMEM)

SMEM = pl.BlockSpec(memory_space=pltpu.SMEM)


def bf16_parts(x):
    top = x.astype(bf16)
    rest = x - top.astype(f32)
    middle = rest.astype(bf16)
    return top, middle, (rest - middle.astype(f32)).astype(bf16)


def dot(a, b, dims=((1,), (0,))):
    return lax.dot_general(a, b, (dims, ((), ())), preferred_element_type=f32)


def dot_f32(a, b, dims=((1,), (0,))):
    return lax.dot_general(
        a, b, (dims, ((), ())), precision=lax.Precision.HIGHEST, preferred_element_type=f32
    )


def pack_kernel(slab, gain, diag, out):
    size = BLOCK
    out[0:size, :] = slab[0:size, :]
    rows = [*bf16_parts(gain[0:1, :]), *bf16_parts(diag[0:1, :])]
    rows.append(jnp.zeros((out.shape[0] - size - len(rows), size), bf16))
    out[size:, :] = jnp.concatenate(rows, axis=0)


def image_kernel(scale, which_ref, coef_ref, offset_ref, gathered, packed, gain_ref, diag_ref, first, second, share, scaled, gains, diags):
    modes = gathered.shape[0]
    size = BLOCK
    tiles = gain_ref.shape[0]
    rows = tiles * size
    split = first.shape[0]
    wide = size + 2 * BAND
    row = lax.broadcasted_iota(jnp.int32, (size, wide), 0)
    column = lax.broadcasted_iota(jnp.int32, (size, wide), 1)
    distance = jnp.abs(column - row - BAND)
    band = jnp.zeros((size, wide), f32)
    for j in range(NOFF):
        band = band + jnp.where(distance == offset_ref[j], coef_ref[j], 0.0)
    parts = bf16_parts(band)
    across_end = jnp.logical_and(which_ref[1] != 0, (row < size - BAND) != (column < size))
    last_parts = bf16_parts(jnp.where(across_end, 0.0, band))
    tail = packed[size:, :].astype(f32)
    next_gain = tail[0:1, :] + tail[1:2, :] + tail[2:3, :]
    next_diag = tail[3:4, :] + tail[4:5, :] + tail[5:6, :]
    for ref, own, extra in ((gains, gain_ref, next_gain), (diags, diag_ref, next_diag)):
        filler = jnp.zeros((8 - (tiles + 1) % 8, size), f32)
        turned = jnp.transpose(jnp.concatenate([own[...], extra, filler], axis=0))
        for i in range(tiles + 1):
            ref[i * size : (i + 1) * size, :] = jnp.broadcast_to(turned[:, i : i + 1], (size, size))
    for m in range(modes):
        lanes = slice(m * size, (m + 1) * size)
        scaled[:, lanes] = (gains[...] * gathered[m].astype(f32)).astype(bf16)
    for i in range(tiles):
        rows_in = scaled[i * size : i * size + wide, :]
        p = last_parts if i == tiles - 1 else parts
        neighbour = dot(p[0], rows_in) + dot(p[1], rows_in) + dot(p[2], rows_in)
        here = slice(BAND + i * size, BAND + (i + 1) * size)
        gain, diag = gains[here, :], diags[here, :]
        for m in range(modes):
            lanes = slice(m * size, (m + 1) * size)
            value = (diag * gathered[m, here, :].astype(f32) + gain * neighbour[:, lanes]).astype(bf16)
            for image, low, high in ((first, 0, split), (second, split, rows)):
                a, b = max(low, i * size), min(high, (i + 1) * size)
                if a < b:
                    image[a - low : b - low, lanes] = value[a - i * size : b - i * size, :]

    def block(s):
        i, j = which_ref[2 + 2 * s], which_ref[3 + 2 * s]
        total = jnp.zeros((size, size), f32)
        for image, at in ((first, BAND), (second, BAND + split)):
            image_i = image[:, pl.ds(pl.multiple_of(i * size, size), size)]
            image_j = image[:, pl.ds(pl.multiple_of(j * size, size), size)]
            slab_i = gathered[i, at : at + image.shape[0], :]
            slab_j = gathered[j, at : at + image.shape[0], :]
            over_rows = ((0,), (0,))
            total = total + dot(image_i, slab_j, over_rows) + dot(slab_i, image_j, over_rows)
        return total * scale

    row = lax.broadcasted_iota(jnp.int32, (size, size), 0)
    column = lax.broadcasted_iota(jnp.int32, (size, size), 1)
    upper = block(1)
    share[0:size, :] = jnp.where(row >= column, block(0), upper)
    share[size : 2 * size, :] = block(2)
    diagonal = jnp.sum(jnp.where(row == column, upper, 0.0), axis=0, keepdims=True)
    share[2 * size :, :] = jnp.broadcast_to(diagonal, (8, size))


def lanes_of(x, t):
    return jnp.broadcast_to(x[:, t : t + 1], (8, BLOCK))


def rows_of(x, t):
    return jnp.broadcast_to(x[t : t + 1, :], (8, BLOCK))


def inverse_factor(square, depth=3):
    panels = BLOCK // 8
    sub = lax.broadcasted_iota(jnp.int32, (8, BLOCK), 0)
    lane = lax.broadcasted_iota(jnp.int32, (8, BLOCK), 1)
    rows = [square[8 * p : 8 * p + 8, :] for p in range(panels)]
    own = [lanes_of(rows[0], t) for t in range(8)]
    result = []
    for p in range(panels):
        below = range(p + 1, min(panels, p + 1 + depth))
        under = {i: [lanes_of(rows[i], 8 * p + t) for t in range(8)] for i in below}
        ahead = [lanes_of(rows[p + 1], 8 * p + 8 + t) for t in range(8)] if p + 1 < panels else []
        inside = jnp.logical_and(lane >= 8 * p, lane < 8 * p + 8)
        a = jnp.where(inside, (lane == sub + 8 * p).astype(f32), rows[p])
        for i in below:
            rows[i] = jnp.where(inside, 0.0, rows[i])
        pivots = jnp.ones((8, BLOCK), f32)
        inverses = jnp.ones((8, BLOCK), f32)
        for t in range(8):
            pivot = rows_of(own[t], t)
            inverse = 1.0 / pivot
            pivots = jnp.where(sub == t, pivot, pivots)
            inverses = jnp.where(sub == t, inverse, inverses)
            f = jnp.where(sub > t, own[t], 0.0) * inverse
            g = {i: under[i][t] * inverse for i in below}
            for u in range(t + 1, 8):
                u_row = rows_of(own[u], t)
                own[u] = own[u] - f * u_row
                for i in below:
                    under[i][u] = under[i][u] - g[i] * u_row
            for u in range(len(ahead)):
                ahead[u] = ahead[u] - g[p + 1] * rows_of(under[p + 1][t], u)
            a_row = rows_of(a, t)
            if t < 7:
                a = a - f * a_row
            for i in below:
                rows[i] = rows[i] - g[i] * a_row
        result.append(jnp.where(lane < 8 * p + 8, a * lax.rsqrt(pivots), 0.0))
        own = ahead
        rest = p + 1 + depth
        if rest < panels:
            a0, a1, a2 = bf16_parts(a * inverses)
            b0, b1, b2 = bf16_parts(a)
            update = dot(
                jnp.concatenate([a0, a0, a1, a0, a2, a1], axis=0)[:, 8 * rest :],
                jnp.concatenate([b0, b1, b0, b2, b0, b1], axis=0),
                ((0,), (0,)),
            )
            for i in range(rest, panels):
                at = slice(8 * (i - rest), 8 * (i - rest) + 8)
                rows[i] = jnp.where(inside, 0.0, rows[i]) - update[at, :]
    return jnp.concatenate(result, axis=0)


def factor_kernel(which_ref, share, beside, across, opposite, inverse, gram, schur, solved):
    for distance, part in enumerate((share, beside, across, opposite)):
        gram[which_ref[0] ^ distance] = part[...]
    count = inverse.shape[1] // BLOCK
    size = BLOCK
    place = lambda i, j: slice((i * (i + 1) // 2 + j) * size, (i * (i + 1) // 2 + j + 1) * size)
    across = ((1,), (1,))
    row = lax.broadcasted_iota(jnp.int32, (size, size), 0)
    column = lax.broadcasted_iota(jnp.int32, (size, size), 1)
    for m, (one, two, three) in enumerate(SHARES):
        square = gram[m, 0:size, :]
        if one == two:
            schur[place(*one), :] = square
        else:
            turned = jnp.transpose(square)
            schur[place(*one), :] = jnp.where(row >= column, square, turned)
            diagonal = jnp.broadcast_to(gram[m, 2 * size : 2 * size + 1, :], (size, size))
            schur[place(*two), :] = jnp.where(
                row < column, square, jnp.where(row == column, diagonal, turned)
            )
        schur[place(*three), :] = gram[m, size : 2 * size, :]
    solved[...] = jnp.zeros(solved.shape, f32)
    for k in range(count):
        w = inverse_factor(schur[place(k, k), :])
        here = slice(k * size, (k + 1) * size)
        if k:
            solved[here, : k * size] = -dot_f32(w, solved[here, : k * size])
        solved[here, here] = w
        lower = [None] * count
        for i in range(k + 1, count):
            lower[i] = dot_f32(schur[place(i, k), :], w, across)
        for i in range(k + 1, count):
            for j in range(k + 1, i + 1):
                schur[place(i, j), :] = schur[place(i, j), :] - dot_f32(lower[i], lower[j], across)
        for i in range(k + 1, count):
            there = slice(i * size, (i + 1) * size)
            done = (k + 1) * size
            solved[there, :done] = solved[there, :done] + dot_f32(lower[i], solved[here, :done])
    mine = pl.multiple_of(which_ref[0] * size, size)
    inverse[...] = solved[pl.ds(mine, size), :].astype(bf16)


def project_kernel(blocks_ref, counts_ref, low, first, second, high, inverse, shapes, out, basis, picked):
    size = BLOCK
    across = ((1,), (1,))
    at = 0
    for part in (low, first, second, high):
        basis[at : at + part.shape[0], :] = dot(part[...], inverse[...], across).astype(bf16)
        at += part.shape[0]
    for c in range(out.shape[0]):
        for s in range(BMAX):
            start = pl.multiple_of(blocks_ref[BMAX * c + s] * size, size)
            rows = basis[pl.ds(start, size), :]
            picked[s * size : (s + 1) * size, :] = jnp.where(s < counts_ref[c], rows, jnp.zeros_like(rows))
        out[c] = dot(picked[...], shapes[c], ((0,), (0,))).astype(bf16)


def exchange(value, axis, step):
    return lax.ppermute(value, axis, [(i, i ^ step) for i in range(lax.axis_size(axis))])


def sum_over_rows(value):
    step = 1
    while step < lax.axis_size("rows"):
        value = value + exchange(value, "rows", step)
        step *= 2
    return value


def local(
    mode_slab,
    mass_diag,
    mass_gain,
    band_coef,
    band_offsets,
    boundary_blocks,
    boundary_counts,
    boundary_modes,
):
    rows_dev, mode_cols = mode_slab.shape
    modes = lax.axis_size("modes")
    row_devices = lax.axis_size("rows")
    order = mode_cols * modes
    count = order // BLOCK
    per_dev = rows_dev // BLOCK
    rim_rows = per_dev // 2 * BLOCK
    total_rows = rows_dev * row_devices
    assert modes == len(SHARES) and order == modes * BLOCK and mode_cols == BLOCK
    assert rows_dev == 2 * rim_rows and row_devices & (row_devices - 1) == 0
    around = [(i, (i + 1) % row_devices) for i in range(row_devices)]
    back = [(target, source) for source, target in around]
    gain_rows = near(mass_gain.reshape(per_dev, BLOCK))
    diag_rows = near(mass_diag.reshape(per_dev, BLOCK))

    packed = pl.pallas_call(
        pack_kernel,
        out_shape=pltpu.VMEM((BLOCK + 16, mode_cols), bf16),
        in_specs=[VMEM, VMEM, VMEM],
        out_specs=VMEM,
        name="pack",
    )(mode_slab, mass_gain.reshape(per_dev, BLOCK), mass_diag.reshape(per_dev, BLOCK))
    packed = lax.ppermute(packed, "rows", back)
    gathered = lax.all_gather(jnp.concatenate([mode_slab, packed[:BLOCK, :]], axis=0), "modes", axis=0)

    mode_index = lax.axis_index("modes")
    is_last = lax.axis_index("rows") == row_devices - 1
    blocks = jnp.asarray(SHARES, jnp.int32).reshape(modes, -1)[mode_index]
    which = jnp.concatenate([jnp.stack([mode_index, is_last.astype(jnp.int32)]).astype(jnp.int32), blocks])
    extended = rows_dev + BLOCK
    first, second, share = pl.pallas_call(
        lambda *refs: image_kernel(0.5 / total_rows, *refs),
        out_shape=(
            pltpu.VMEM((rim_rows - BAND, order), bf16),
            pltpu.VMEM((rim_rows + BAND, order), bf16),
            pltpu.VMEM((2 * BLOCK + 8, BLOCK), f32),
        ),
        in_specs=[SMEM, SMEM, SMEM, VMEM, VMEM, VMEM, VMEM],
        out_specs=(VMEM, VMEM, VMEM),
        scratch_shapes=[
            pltpu.VMEM((extended, order), bf16),
            pltpu.VMEM((extended, BLOCK), f32),
            pltpu.VMEM((extended, BLOCK), f32),
        ],
        name="image",
    )(which, band_coef, band_offsets, near(gathered), near(packed), gain_rows, diag_rows)

    share = sum_over_rows(share)
    share, one, two = lax.optimization_barrier((share, first, second))
    across = exchange(share, "modes", 2)
    beside = exchange(share, "modes", 1)
    rim_low = lax.ppermute(two, "rows", around)
    rim_high = lax.ppermute(one, "rows", back)
    opposite = exchange(across, "modes", 1)

    inverse = pl.pallas_call(
        factor_kernel,
        out_shape=pltpu.VMEM((BLOCK, order), bf16),
        in_specs=[SMEM, VMEM, VMEM, VMEM, VMEM],
        out_specs=VMEM,
        scratch_shapes=[
            pltpu.VMEM((modes, 2 * BLOCK + 8, BLOCK), f32),
            pltpu.VMEM((count * (count + 1) // 2 * BLOCK, BLOCK), f32),
            pltpu.VMEM((order, order), f32),
        ],
        name="factor",
    )(which, near(share), near(beside), near(across), near(opposite))

    total_blocks = per_dev * row_devices
    window_start = lax.axis_index("rows") * per_dev - per_dev // 2
    local_blocks = jnp.mod(boundary_blocks - window_start, total_blocks).reshape(-1)
    owned, _, width = boundary_modes.shape
    window = per_dev + 2 * (per_dev // 2)
    return pl.pallas_call(
        project_kernel,
        out_shape=jax.ShapeDtypeStruct((owned, mode_cols, width), bf16),
        in_specs=[SMEM, SMEM, VMEM, VMEM, VMEM, VMEM, VMEM, VMEM],
        out_specs=VMEM,
        scratch_shapes=[
            pltpu.VMEM((window * BLOCK, BLOCK), bf16),
            pltpu.VMEM((BMAX * BLOCK, BLOCK), bf16),
        ],
        name="project",
    )(local_blocks, boundary_counts, near(rim_low), near(first), near(second), near(rim_high), near(inverse), near(boundary_modes))


def solution(mesh):
    in_specs = (
        P("rows", "modes"),
        P("rows"),
        P("rows"),
        P(),
        P(),
        P("rows", None),
        P("rows"),
        P("rows", None, None),
    )
    out_specs = P("rows", "modes", None)
    return jax.shard_map(local, mesh=mesh, in_specs=in_specs, out_specs=out_specs, check_vma=False)
```

```python
import jax
import jax.numpy as jnp
from jax import lax
from jax.experimental import pallas as pl
from jax.experimental.pallas import tpu as pltpu
from jax.sharding import PartitionSpec as P

BLOCK = 128
BMAX = 4
NOFF = 4
BAND = 64
SHARES = (
    ((0, 0), (1, 1), (1, 0)),
    ((2, 2), (3, 3), (2, 0)),
    ((2, 1), (2, 1), (3, 0)),
    ((3, 1), (3, 1), (3, 2)),
)

f32 = jnp.float32
bf16 = jnp.bfloat16
VMEM = pl.BlockSpec(memory_space=pltpu.VMEM)


def near(x):
    return pltpu.with_memory_space_constraint(x, pltpu.VMEM)

SMEM = pl.BlockSpec(memory_space=pltpu.SMEM)


def bf16_parts(x):
    top = x.astype(bf16)
    rest = x - top.astype(f32)
    middle = rest.astype(bf16)
    return top, middle, (rest - middle.astype(f32)).astype(bf16)


def dot(a, b, dims=((1,), (0,))):
    return lax.dot_general(a, b, (dims, ((), ())), preferred_element_type=f32)


def dot_f32(a, b, dims=((1,), (0,))):
    a0, a1, a2 = bf16_parts(a)
    b0, b1, b2 = bf16_parts(b)
    return dot(
        jnp.concatenate([a0, a0, a1, a0, a2, a1], axis=dims[0][0]),
        jnp.concatenate([b0, b1, b0, b2, b0, b1], axis=dims[1][0]),
        dims,
    )


def pack_kernel(slab, gain, diag, out):
    size = BLOCK
    out[0:size, :] = slab[0:size, :]
    rows = [*bf16_parts(gain[0:1, :]), *bf16_parts(diag[0:1, :])]
    rows.append(jnp.zeros((out.shape[0] - size - len(rows), size), bf16))
    out[size:, :] = jnp.concatenate(rows, axis=0)


def image_kernel(scale, which_ref, coef_ref, offset_ref, *refs):
    slabs, edges = refs[:4], refs[4:8]
    gain_ref, diag_ref, first, second, share, gathered, scaled, gains, diags = refs[8:]
    modes = gathered.shape[0]
    size = BLOCK
    tiles = gain_ref.shape[0]
    rows = tiles * size
    for distance in range(modes):
        m = which_ref[0] ^ distance
        gathered[m, 0:rows, :] = slabs[distance][...]
        gathered[m, rows:, :] = edges[distance][0:size, :]
    split = first.shape[0]
    wide = size + 2 * BAND
    row = lax.broadcasted_iota(jnp.int32, (size, wide), 0)
    column = lax.broadcasted_iota(jnp.int32, (size, wide), 1)
    distance = jnp.abs(column - row - BAND)
    band = jnp.zeros((size, wide), f32)
    for j in range(NOFF):
        band = band + jnp.where(distance == offset_ref[j], coef_ref[j], 0.0)
    parts = bf16_parts(band)
    across_end = jnp.logical_and(which_ref[1] != 0, (row < size - BAND) != (column < size))
    last_parts = bf16_parts(jnp.where(across_end, 0.0, band))
    tail = edges[0][size:, :].astype(f32)
    next_gain = tail[0:1, :] + tail[1:2, :] + tail[2:3, :]
    next_diag = tail[3:4, :] + tail[4:5, :] + tail[5:6, :]
    for ref, own, extra in ((gains, gain_ref, next_gain), (diags, diag_ref, next_diag)):
        filler = jnp.zeros((8 - (tiles + 1) % 8, size), f32)
        turned = jnp.transpose(jnp.concatenate([own[...], extra, filler], axis=0))
        for i in range(tiles + 1):
            ref[i * size : (i + 1) * size, :] = jnp.broadcast_to(turned[:, i : i + 1], (size, size))
    for m in range(modes):
        lanes = slice(m * size, (m + 1) * size)
        scaled[:, lanes] = (gains[...] * gathered[m].astype(f32)).astype(bf16)
    for i in range(tiles):
        rows_in = scaled[i * size : i * size + wide, :]
        p = last_parts if i == tiles - 1 else parts
        neighbour = dot(p[0], rows_in) + dot(p[1], rows_in) + dot(p[2], rows_in)
        here = slice(BAND + i * size, BAND + (i + 1) * size)
        gain, diag = gains[here, :], diags[here, :]
        for m in range(modes):
            lanes = slice(m * size, (m + 1) * size)
            value = (diag * gathered[m, here, :].astype(f32) + gain * neighbour[:, lanes]).astype(bf16)
            for image, low, high in ((first, 0, split), (second, split, rows)):
                a, b = max(low, i * size), min(high, (i + 1) * size)
                if a < b:
                    image[a - low : b - low, lanes] = value[a - i * size : b - i * size, :]

    def block(s):
        i, j = which_ref[2 + 2 * s], which_ref[3 + 2 * s]
        total = jnp.zeros((size, size), f32)
        for image, at in ((first, BAND), (second, BAND + split)):
            image_i = image[:, pl.ds(pl.multiple_of(i * size, size), size)]
            image_j = image[:, pl.ds(pl.multiple_of(j * size, size), size)]
            slab_i = gathered[i, at : at + image.shape[0], :]
            slab_j = gathered[j, at : at + image.shape[0], :]
            over_rows = ((0,), (0,))
            total = total + dot(image_i, slab_j, over_rows) + dot(slab_i, image_j, over_rows)
        return total * scale

    row = lax.broadcasted_iota(jnp.int32, (size, size), 0)
    column = lax.broadcasted_iota(jnp.int32, (size, size), 1)
    upper = block(1)
    share[0:size, :] = jnp.where(row >= column, block(0), upper)
    share[size : 2 * size, :] = block(2)
    diagonal = jnp.sum(jnp.where(row == column, upper, 0.0), axis=0, keepdims=True)
    share[2 * size :, :] = jnp.broadcast_to(diagonal, (8, size))


def lanes_of(x, t):
    return jnp.broadcast_to(x[:, t : t + 1], (8, BLOCK))


def rows_of(x, t):
    return jnp.broadcast_to(x[t : t + 1, :], (8, BLOCK))


def inverse_factor(square, depth=3):
    panels = BLOCK // 8
    sub = lax.broadcasted_iota(jnp.int32, (8, BLOCK), 0)
    lane = lax.broadcasted_iota(jnp.int32, (8, BLOCK), 1)
    rows = [square[8 * p : 8 * p + 8, :] for p in range(panels)]
    own = [lanes_of(rows[0], t) for t in range(8)]
    result = []
    for p in range(panels):
        below = range(p + 1, min(panels, p + 1 + depth))
        under = {i: [lanes_of(rows[i], 8 * p + t) for t in range(8)] for i in below}
        ahead = [lanes_of(rows[p + 1], 8 * p + 8 + t) for t in range(8)] if p + 1 < panels else []
        inside = jnp.logical_and(lane >= 8 * p, lane < 8 * p + 8)
        a = jnp.where(inside, (lane == sub + 8 * p).astype(f32), rows[p])
        for i in below:
            rows[i] = jnp.where(inside, 0.0, rows[i])
        pivots = jnp.ones((8, BLOCK), f32)
        inverses = jnp.ones((8, BLOCK), f32)
        for t in range(8):
            pivot = rows_of(own[t], t)
            inverse = 1.0 / pivot
            pivots = jnp.where(sub == t, pivot, pivots)
            inverses = jnp.where(sub == t, inverse, inverses)
            f = jnp.where(sub > t, own[t], 0.0) * inverse
            g = {i: under[i][t] * inverse for i in below}
            for u in range(t + 1, 8):
                u_row = rows_of(own[u], t)
                own[u] = own[u] - f * u_row
                for i in below:
                    under[i][u] = under[i][u] - g[i] * u_row
            for u in range(len(ahead)):
                ahead[u] = ahead[u] - g[p + 1] * rows_of(under[p + 1][t], u)
            a_row = rows_of(a, t)
            if t < 7:
                a = a - f * a_row
            for i in below:
                rows[i] = rows[i] - g[i] * a_row
        result.append(jnp.where(lane < 8 * p + 8, a * lax.rsqrt(pivots), 0.0))
        own = ahead
        rest = p + 1 + depth
        if rest < panels:
            a0, a1, a2 = bf16_parts(a * inverses)
            b0, b1, b2 = bf16_parts(a)
            update = dot(
                jnp.concatenate([a0, a0, a1, a0, a2, a1], axis=0)[:, 8 * rest :],
                jnp.concatenate([b0, b1, b0, b2, b0, b1], axis=0),
                ((0,), (0,)),
            )
            for i in range(rest, panels):
                at = slice(8 * (i - rest), 8 * (i - rest) + 8)
                rows[i] = jnp.where(inside, 0.0, rows[i]) - update[at, :]
    return jnp.concatenate(result, axis=0)


def factor_kernel(which_ref, share, beside, across, opposite, inverse, gram, schur, solved):
    for distance, part in enumerate((share, beside, across, opposite)):
        gram[which_ref[0] ^ distance] = part[...]
    count = inverse.shape[1] // BLOCK
    size = BLOCK
    place = lambda i, j: slice((i * (i + 1) // 2 + j) * size, (i * (i + 1) // 2 + j + 1) * size)
    across = ((1,), (1,))
    row = lax.broadcasted_iota(jnp.int32, (size, size), 0)
    column = lax.broadcasted_iota(jnp.int32, (size, size), 1)
    for m, (one, two, three) in enumerate(SHARES):
        square = gram[m, 0:size, :]
        if one == two:
            schur[place(*one), :] = square
        else:
            turned = jnp.transpose(square)
            schur[place(*one), :] = jnp.where(row >= column, square, turned)
            diagonal = jnp.broadcast_to(gram[m, 2 * size : 2 * size + 1, :], (size, size))
            schur[place(*two), :] = jnp.where(
                row < column, square, jnp.where(row == column, diagonal, turned)
            )
        schur[place(*three), :] = gram[m, size : 2 * size, :]
    solved[...] = jnp.zeros(solved.shape, f32)
    for k in range(count):
        w = inverse_factor(schur[place(k, k), :])
        here = slice(k * size, (k + 1) * size)
        if k:
            solved[here, : k * size] = -dot_f32(w, solved[here, : k * size])
        solved[here, here] = w
        lower = [None] * count
        for i in range(k + 1, count):
            lower[i] = dot_f32(schur[place(i, k), :], w, across)
        for i in range(k + 1, count):
            for j in range(k + 1, i + 1):
                schur[place(i, j), :] = schur[place(i, j), :] - dot_f32(lower[i], lower[j], across)
        for i in range(k + 1, count):
            there = slice(i * size, (i + 1) * size)
            done = (k + 1) * size
            solved[there, :done] = solved[there, :done] + dot_f32(lower[i], solved[here, :done])
    mine = pl.multiple_of(which_ref[0] * size, size)
    inverse[...] = solved[pl.ds(mine, size), :].astype(bf16)


def project_kernel(blocks_ref, counts_ref, low, first, second, high, inverse, shapes, out, basis, picked):
    size = BLOCK
    across = ((1,), (1,))
    at = 0
    for part in (low, first, second, high):
        basis[at : at + part.shape[0], :] = dot(part[...], inverse[...], across).astype(bf16)
        at += part.shape[0]
    for c in range(out.shape[0]):
        for s in range(BMAX):
            start = pl.multiple_of(blocks_ref[BMAX * c + s] * size, size)
            rows = basis[pl.ds(start, size), :]
            picked[s * size : (s + 1) * size, :] = jnp.where(s < counts_ref[c], rows, jnp.zeros_like(rows))
        out[c] = dot(picked[...], shapes[c], ((0,), (0,))).astype(bf16)


def exchange(value, axis, step):
    return lax.ppermute(value, axis, [(i, i ^ step) for i in range(lax.axis_size(axis))])


def from_modes(value):
    across = exchange(value, "modes", 2)
    beside = exchange(value, "modes", 1)
    return value, beside, across, exchange(across, "modes", 1)


def sum_over_rows(value):
    step = 1
    while step < lax.axis_size("rows"):
        value = value + exchange(value, "rows", step)
        step *= 2
    return value


def local(
    mode_slab,
    mass_diag,
    mass_gain,
    band_coef,
    band_offsets,
    boundary_blocks,
    boundary_counts,
    boundary_modes,
):
    rows_dev, mode_cols = mode_slab.shape
    modes = lax.axis_size("modes")
    row_devices = lax.axis_size("rows")
    order = mode_cols * modes
    count = order // BLOCK
    per_dev = rows_dev // BLOCK
    rim_rows = per_dev // 2 * BLOCK
    total_rows = rows_dev * row_devices
    assert modes == len(SHARES) and order == modes * BLOCK and mode_cols == BLOCK
    assert rows_dev == 2 * rim_rows and row_devices & (row_devices - 1) == 0
    around = [(i, (i + 1) % row_devices) for i in range(row_devices)]
    back = [(target, source) for source, target in around]
    gain_rows = near(mass_gain.reshape(per_dev, BLOCK))
    diag_rows = near(mass_diag.reshape(per_dev, BLOCK))

    packed = pl.pallas_call(
        pack_kernel,
        out_shape=pltpu.VMEM((BLOCK + 16, mode_cols), bf16),
        in_specs=[VMEM, VMEM, VMEM],
        out_specs=VMEM,
        name="pack",
    )(mode_slab, mass_gain.reshape(per_dev, BLOCK), mass_diag.reshape(per_dev, BLOCK))
    edge = lax.ppermute(packed, "rows", back)
    slabs = from_modes(mode_slab)
    edges = from_modes(edge)

    mode_index = lax.axis_index("modes")
    is_last = lax.axis_index("rows") == row_devices - 1
    blocks = jnp.asarray(SHARES, jnp.int32).reshape(modes, -1)[mode_index]
    which = jnp.concatenate([jnp.stack([mode_index, is_last.astype(jnp.int32)]).astype(jnp.int32), blocks])
    extended = rows_dev + BLOCK
    first, second, share = pl.pallas_call(
        lambda *refs: image_kernel(0.5 / total_rows, *refs),
        out_shape=(
            pltpu.VMEM((rim_rows - BAND, order), bf16),
            pltpu.VMEM((rim_rows + BAND, order), bf16),
            pltpu.VMEM((2 * BLOCK + 8, BLOCK), f32),
        ),
        in_specs=[SMEM, SMEM, SMEM] + [VMEM] * 10,
        out_specs=(VMEM, VMEM, VMEM),
        scratch_shapes=[
            pltpu.VMEM((modes, extended, BLOCK), bf16),
            pltpu.VMEM((extended, order), bf16),
            pltpu.VMEM((extended, BLOCK), f32),
            pltpu.VMEM((extended, BLOCK), f32),
        ],
        name="image",
    )(which, band_coef, band_offsets, *map(near, slabs), *map(near, edges), gain_rows, diag_rows)

    share = sum_over_rows(share)
    share, one, two = lax.optimization_barrier((share, first, second))
    across = exchange(share, "modes", 2)
    beside = exchange(share, "modes", 1)
    rim_low = lax.ppermute(two, "rows", around)
    rim_high = lax.ppermute(one, "rows", back)
    opposite = exchange(across, "modes", 1)

    inverse = pl.pallas_call(
        factor_kernel,
        out_shape=pltpu.VMEM((BLOCK, order), bf16),
        in_specs=[SMEM, VMEM, VMEM, VMEM, VMEM],
        out_specs=VMEM,
        scratch_shapes=[
            pltpu.VMEM((modes, 2 * BLOCK + 8, BLOCK), f32),
            pltpu.VMEM((count * (count + 1) // 2 * BLOCK, BLOCK), f32),
            pltpu.VMEM((order, order), f32),
        ],
        name="factor",
    )(which, near(share), near(beside), near(across), near(opposite))

    total_blocks = per_dev * row_devices
    window_start = lax.axis_index("rows") * per_dev - per_dev // 2
    local_blocks = jnp.mod(boundary_blocks - window_start, total_blocks).reshape(-1)
    owned, _, width = boundary_modes.shape
    window = per_dev + 2 * (per_dev // 2)
    return pl.pallas_call(
        project_kernel,
        out_shape=jax.ShapeDtypeStruct((owned, mode_cols, width), bf16),
        in_specs=[SMEM, SMEM, VMEM, VMEM, VMEM, VMEM, VMEM, VMEM],
        out_specs=VMEM,
        scratch_shapes=[
            pltpu.VMEM((window * BLOCK, BLOCK), bf16),
            pltpu.VMEM((BMAX * BLOCK, BLOCK), bf16),
        ],
        name="project",
    )(local_blocks, boundary_counts, near(rim_low), near(first), near(second), near(rim_high), near(inverse), near(boundary_modes))


def solution(mesh):
    in_specs = (
        P("rows", "modes"),
        P("rows"),
        P("rows"),
        P(),
        P(),
        P("rows", None),
        P("rows"),
        P("rows", None, None),
    )
    out_specs = P("rows", "modes", None)
    return jax.shard_map(local, mesh=mesh, in_specs=in_specs, out_specs=out_specs, check_vma=False)
```

```python
import jax
import jax.numpy as jnp
from jax import lax
from jax.experimental import pallas as pl
from jax.experimental.pallas import tpu as pltpu
from jax.sharding import PartitionSpec as P

BLOCK = 128
BMAX = 4
NOFF = 4
BAND = 64
SHARES = (
    ((0, 0), (1, 1), (1, 0)),
    ((2, 2), (3, 3), (2, 0)),
    ((2, 1), (2, 1), (3, 0)),
    ((3, 1), (3, 1), (3, 2)),
)

f32 = jnp.float32
bf16 = jnp.bfloat16
VMEM = pl.BlockSpec(memory_space=pltpu.VMEM)


def near(x):
    return pltpu.with_memory_space_constraint(x, pltpu.VMEM)

SMEM = pl.BlockSpec(memory_space=pltpu.SMEM)


def bf16_parts(x):
    top = x.astype(bf16)
    rest = x - top.astype(f32)
    middle = rest.astype(bf16)
    return top, middle, (rest - middle.astype(f32)).astype(bf16)


def dot(a, b, dims=((1,), (0,))):
    return lax.dot_general(a, b, (dims, ((), ())), preferred_element_type=f32)


def dot_f32(a, b, dims=((1,), (0,))):
    a0, a1, a2 = bf16_parts(a)
    b0, b1, b2 = bf16_parts(b)
    return dot(
        jnp.concatenate([a0, a0, a1, a0, a2, a1], axis=dims[0][0]),
        jnp.concatenate([b0, b1, b0, b2, b0, b1], axis=dims[1][0]),
        dims,
    )


def pack_kernel(slab, gain, diag, out):
    size = BLOCK
    out[0:size, :] = slab[0:size, :]
    rows = [*bf16_parts(gain[0:1, :]), *bf16_parts(diag[0:1, :])]
    rows.append(jnp.zeros((out.shape[0] - size - len(rows), size), bf16))
    out[size:, :] = jnp.concatenate(rows, axis=0)


def image_kernel(scale, which_ref, coef_ref, offset_ref, *refs):
    slabs, edges = refs[:4], refs[4:8]
    gain_ref, diag_ref, first, second, share, gathered, scaled, gains, diags = refs[8:]
    modes = gathered.shape[0]
    size = BLOCK
    tiles = gain_ref.shape[0]
    rows = tiles * size
    for distance in range(modes):
        m = which_ref[0] ^ distance
        gathered[m, 0:rows, :] = slabs[distance][...]
        gathered[m, rows:, :] = edges[distance][0:size, :]
    split = first.shape[0]
    wide = size + 2 * BAND
    row = lax.broadcasted_iota(jnp.int32, (size, wide), 0)
    column = lax.broadcasted_iota(jnp.int32, (size, wide), 1)
    distance = jnp.abs(column - row - BAND)
    band = jnp.zeros((size, wide), f32)
    for j in range(NOFF):
        band = band + jnp.where(distance == offset_ref[j], coef_ref[j], 0.0)
    parts = bf16_parts(band)
    across_end = jnp.logical_and(which_ref[1] != 0, (row < size - BAND) != (column < size))
    last_parts = bf16_parts(jnp.where(across_end, 0.0, band))
    tail = edges[0][size:, :].astype(f32)
    next_gain = tail[0:1, :] + tail[1:2, :] + tail[2:3, :]
    next_diag = tail[3:4, :] + tail[4:5, :] + tail[5:6, :]
    for ref, own, extra in ((gains, gain_ref, next_gain), (diags, diag_ref, next_diag)):
        filler = jnp.zeros((8 - (tiles + 1) % 8, size), f32)
        turned = jnp.transpose(jnp.concatenate([own[...], extra, filler], axis=0))
        for i in range(tiles + 1):
            ref[i * size : (i + 1) * size, :] = jnp.broadcast_to(turned[:, i : i + 1], (size, size))
    for m in range(modes):
        lanes = slice(m * size, (m + 1) * size)
        scaled[:, lanes] = (gains[...] * gathered[m].astype(f32)).astype(bf16)
    for i in range(tiles):
        rows_in = scaled[i * size : i * size + wide, :]
        p = last_parts if i == tiles - 1 else parts
        neighbour = dot(p[0], rows_in) + dot(p[1], rows_in) + dot(p[2], rows_in)
        here = slice(BAND + i * size, BAND + (i + 1) * size)
        gain, diag = gains[here, :], diags[here, :]
        for m in range(modes):
            lanes = slice(m * size, (m + 1) * size)
            value = (diag * gathered[m, here, :].astype(f32) + gain * neighbour[:, lanes]).astype(bf16)
            for image, low, high in ((first, 0, split), (second, split, rows)):
                a, b = max(low, i * size), min(high, (i + 1) * size)
                if a < b:
                    image[a - low : b - low, lanes] = value[a - i * size : b - i * size, :]

    def block(s):
        i, j = which_ref[2 + 2 * s], which_ref[3 + 2 * s]
        total = jnp.zeros((size, size), f32)
        for image, at in ((first, BAND), (second, BAND + split)):
            image_i = image[:, pl.ds(pl.multiple_of(i * size, size), size)]
            image_j = image[:, pl.ds(pl.multiple_of(j * size, size), size)]
            slab_i = gathered[i, at : at + image.shape[0], :]
            slab_j = gathered[j, at : at + image.shape[0], :]
            over_rows = ((0,), (0,))
            total = total + dot(image_i, slab_j, over_rows) + dot(slab_i, image_j, over_rows)
        return total * scale

    row = lax.broadcasted_iota(jnp.int32, (size, size), 0)
    column = lax.broadcasted_iota(jnp.int32, (size, size), 1)
    upper = block(1)
    share[0:size, :] = jnp.where(row >= column, block(0), upper)
    share[size : 2 * size, :] = block(2)
    diagonal = jnp.sum(jnp.where(row == column, upper, 0.0), axis=0, keepdims=True)
    share[2 * size :, :] = jnp.broadcast_to(diagonal, (8, size))


def lanes_of(x, t):
    return jnp.broadcast_to(x[:, t : t + 1], (8, BLOCK))


def rows_of(x, t):
    return jnp.broadcast_to(x[t : t + 1, :], (8, BLOCK))


def inverse_factor(square, depth=3):
    panels = BLOCK // 8
    sub = lax.broadcasted_iota(jnp.int32, (8, BLOCK), 0)
    lane = lax.broadcasted_iota(jnp.int32, (8, BLOCK), 1)
    rows = [square[8 * p : 8 * p + 8, :] for p in range(panels)]
    own = [lanes_of(rows[0], t) for t in range(8)]
    result = []
    for p in range(panels):
        below = range(p + 1, min(panels, p + 1 + depth))
        under = {i: [lanes_of(rows[i], 8 * p + t) for t in range(8)] for i in below}
        ahead = [lanes_of(rows[p + 1], 8 * p + 8 + t) for t in range(8)] if p + 1 < panels else []
        inside = jnp.logical_and(lane >= 8 * p, lane < 8 * p + 8)
        a = jnp.where(inside, (lane == sub + 8 * p).astype(f32), rows[p])
        for i in below:
            rows[i] = jnp.where(inside, 0.0, rows[i])
        pivots = jnp.ones((8, BLOCK), f32)
        inverses = jnp.ones((8, BLOCK), f32)
        for t in range(8):
            pivot = rows_of(own[t], t)
            inverse = 1.0 / pivot
            pivots = jnp.where(sub == t, pivot, pivots)
            inverses = jnp.where(sub == t, inverse, inverses)
            f = jnp.where(sub > t, own[t], 0.0) * inverse
            g = {i: under[i][t] * inverse for i in below}
            for u in range(t + 1, 8):
                u_row = rows_of(own[u], t)
                own[u] = own[u] - f * u_row
                for i in below:
                    under[i][u] = under[i][u] - g[i] * u_row
            for u in range(len(ahead)):
                ahead[u] = ahead[u] - g[p + 1] * rows_of(under[p + 1][t], u)
            a_row = rows_of(a, t)
            if t < 7:
                a = a - f * a_row
            for i in below:
                rows[i] = rows[i] - g[i] * a_row
        result.append(jnp.where(lane < 8 * p + 8, a * lax.rsqrt(pivots), 0.0))
        own = ahead
        rest = p + 1 + depth
        if rest < panels:
            a0, a1, a2 = bf16_parts(a * inverses)
            b0, b1, b2 = bf16_parts(a)
            update = dot(
                jnp.concatenate([a0, a0, a1, a0, a2, a1], axis=0)[:, 8 * rest :],
                jnp.concatenate([b0, b1, b0, b2, b0, b1], axis=0),
                ((0,), (0,)),
            )
            for i in range(rest, panels):
                at = slice(8 * (i - rest), 8 * (i - rest) + 8)
                rows[i] = jnp.where(inside, 0.0, rows[i]) - update[at, :]
    return jnp.concatenate(result, axis=0)


def factor_kernel(which_ref, share, beside, across, opposite, inverse, gram, schur, solved):
    for distance, part in enumerate((share, beside, across, opposite)):
        gram[which_ref[0] ^ distance] = part[...]
    count = inverse.shape[1] // BLOCK
    size = BLOCK
    place = lambda i, j: slice((i * (i + 1) // 2 + j) * size, (i * (i + 1) // 2 + j + 1) * size)
    across = ((1,), (1,))
    row = lax.broadcasted_iota(jnp.int32, (size, size), 0)
    column = lax.broadcasted_iota(jnp.int32, (size, size), 1)
    for m, (one, two, three) in enumerate(SHARES):
        square = gram[m, 0:size, :]
        if one == two:
            schur[place(*one), :] = square
        else:
            turned = jnp.transpose(square)
            schur[place(*one), :] = jnp.where(row >= column, square, turned)
            diagonal = jnp.broadcast_to(gram[m, 2 * size : 2 * size + 1, :], (size, size))
            schur[place(*two), :] = jnp.where(
                row < column, square, jnp.where(row == column, diagonal, turned)
            )
        schur[place(*three), :] = gram[m, size : 2 * size, :]
    solved[...] = jnp.zeros(solved.shape, f32)
    for k in range(count):
        w = inverse_factor(schur[place(k, k), :])
        here = slice(k * size, (k + 1) * size)
        if k:
            solved[here, : k * size] = -dot_f32(w, solved[here, : k * size])
        solved[here, here] = w
        lower = [None] * count
        for i in range(k + 1, count):
            lower[i] = dot_f32(schur[place(i, k), :], w, across)
        for i in range(k + 1, count):
            for j in range(k + 1, i + 1):
                schur[place(i, j), :] = schur[place(i, j), :] - dot_f32(lower[i], lower[j], across)
        for i in range(k + 1, count):
            there = slice(i * size, (i + 1) * size)
            done = (k + 1) * size
            solved[there, :done] = solved[there, :done] + dot_f32(lower[i], solved[here, :done])
    mine = pl.multiple_of(which_ref[0] * size, size)
    inverse[...] = solved[pl.ds(mine, size), :].astype(bf16)


def project_kernel(blocks_ref, counts_ref, low, first, second, high, inverse, shapes, out, basis, picked):
    size = BLOCK
    across = ((1,), (1,))
    at = 0
    for part in (low, first, second, high):
        basis[at : at + part.shape[0], :] = dot(part[...], inverse[...], across).astype(bf16)
        at += part.shape[0]
    for c in range(out.shape[0]):
        for s in range(BMAX):
            start = pl.multiple_of(blocks_ref[BMAX * c + s] * size, size)
            rows = basis[pl.ds(start, size), :]
            picked[s * size : (s + 1) * size, :] = jnp.where(s < counts_ref[c], rows, jnp.zeros_like(rows))
        out[c] = dot(picked[...], shapes[c], ((0,), (0,))).astype(bf16)


def exchange(value, axis, step):
    return lax.ppermute(value, axis, [(i, i ^ step) for i in range(lax.axis_size(axis))])


def from_modes(value):
    across = exchange(value, "modes", 2)
    beside = exchange(value, "modes", 1)
    return value, beside, across, exchange(across, "modes", 1)


def sum_over_rows(value):
    step = 1
    while step < lax.axis_size("rows"):
        value = value + exchange(value, "rows", step)
        step *= 2
    return value


def local(
    mode_slab,
    mass_diag,
    mass_gain,
    band_coef,
    band_offsets,
    boundary_blocks,
    boundary_counts,
    boundary_modes,
):
    rows_dev, mode_cols = mode_slab.shape
    modes = lax.axis_size("modes")
    row_devices = lax.axis_size("rows")
    order = mode_cols * modes
    count = order // BLOCK
    per_dev = rows_dev // BLOCK
    rim_rows = per_dev // 2 * BLOCK
    total_rows = rows_dev * row_devices
    assert modes == len(SHARES) and order == modes * BLOCK and mode_cols == BLOCK
    assert rows_dev == 2 * rim_rows and row_devices & (row_devices - 1) == 0
    around = [(i, (i + 1) % row_devices) for i in range(row_devices)]
    back = [(target, source) for source, target in around]
    gain_rows = near(mass_gain.reshape(per_dev, BLOCK))
    diag_rows = near(mass_diag.reshape(per_dev, BLOCK))

    packed = pl.pallas_call(
        pack_kernel,
        out_shape=pltpu.VMEM((BLOCK + 16, mode_cols), bf16),
        in_specs=[VMEM, VMEM, VMEM],
        out_specs=VMEM,
        name="pack",
    )(mode_slab, mass_gain.reshape(per_dev, BLOCK), mass_diag.reshape(per_dev, BLOCK))
    edge = lax.ppermute(packed, "rows", back)
    slabs = from_modes(mode_slab)
    edges = [edge] + [exchange(edge, "modes", d) for d in (1, 2, 3)]

    mode_index = lax.axis_index("modes")
    is_last = lax.axis_index("rows") == row_devices - 1
    blocks = jnp.asarray(SHARES, jnp.int32).reshape(modes, -1)[mode_index]
    which = jnp.concatenate([jnp.stack([mode_index, is_last.astype(jnp.int32)]).astype(jnp.int32), blocks])
    extended = rows_dev + BLOCK
    first, second, share = pl.pallas_call(
        lambda *refs: image_kernel(0.5 / total_rows, *refs),
        out_shape=(
            pltpu.VMEM((rim_rows - BAND, order), bf16),
            pltpu.VMEM((rim_rows + BAND, order), bf16),
            pltpu.VMEM((2 * BLOCK + 8, BLOCK), f32),
        ),
        in_specs=[SMEM, SMEM, SMEM] + [VMEM] * 10,
        out_specs=(VMEM, VMEM, VMEM),
        scratch_shapes=[
            pltpu.VMEM((modes, extended, BLOCK), bf16),
            pltpu.VMEM((extended, order), bf16),
            pltpu.VMEM((extended, BLOCK), f32),
            pltpu.VMEM((extended, BLOCK), f32),
        ],
        name="image",
    )(which, band_coef, band_offsets, *map(near, slabs), *map(near, edges), gain_rows, diag_rows)

    share = sum_over_rows(share)
    share, one, two = lax.optimization_barrier((share, first, second))
    across = exchange(share, "modes", 2)
    beside = exchange(share, "modes", 1)
    rim_low = lax.ppermute(two, "rows", around)
    rim_high = lax.ppermute(one, "rows", back)
    opposite = exchange(across, "modes", 1)

    inverse = pl.pallas_call(
        factor_kernel,
        out_shape=pltpu.VMEM((BLOCK, order), bf16),
        in_specs=[SMEM, VMEM, VMEM, VMEM, VMEM],
        out_specs=VMEM,
        scratch_shapes=[
            pltpu.VMEM((modes, 2 * BLOCK + 8, BLOCK), f32),
            pltpu.VMEM((count * (count + 1) // 2 * BLOCK, BLOCK), f32),
            pltpu.VMEM((order, order), f32),
        ],
        name="factor",
    )(which, near(share), near(beside), near(across), near(opposite))

    total_blocks = per_dev * row_devices
    window_start = lax.axis_index("rows") * per_dev - per_dev // 2
    local_blocks = jnp.mod(boundary_blocks - window_start, total_blocks).reshape(-1)
    owned, _, width = boundary_modes.shape
    window = per_dev + 2 * (per_dev // 2)
    return pl.pallas_call(
        project_kernel,
        out_shape=jax.ShapeDtypeStruct((owned, mode_cols, width), bf16),
        in_specs=[SMEM, SMEM, VMEM, VMEM, VMEM, VMEM, VMEM, VMEM],
        out_specs=VMEM,
        scratch_shapes=[
            pltpu.VMEM((window * BLOCK, BLOCK), bf16),
            pltpu.VMEM((BMAX * BLOCK, BLOCK), bf16),
        ],
        name="project",
    )(local_blocks, boundary_counts, near(rim_low), near(first), near(second), near(rim_high), near(inverse), near(boundary_modes))


def solution(mesh):
    in_specs = (
        P("rows", "modes"),
        P("rows"),
        P("rows"),
        P(),
        P(),
        P("rows", None),
        P("rows"),
        P("rows", None, None),
    )
    out_specs = P("rows", "modes", None)
    return jax.shard_map(local, mesh=mesh, in_specs=in_specs, out_specs=out_specs, check_vma=False)
```

```python
import jax
import jax.numpy as jnp
from jax import lax
from jax.experimental import pallas as pl
from jax.experimental.pallas import tpu as pltpu
from jax.sharding import PartitionSpec as P

BLOCK = 128
BMAX = 4
NOFF = 4
BAND = 64
SHARES = (
    ((0, 0), (1, 1), (1, 0)),
    ((2, 2), (3, 3), (2, 0)),
    ((2, 1), (2, 1), (3, 0)),
    ((3, 1), (3, 1), (3, 2)),
)

f32 = jnp.float32
bf16 = jnp.bfloat16
VMEM = pl.BlockSpec(memory_space=pltpu.VMEM)


def near(x):
    return pltpu.with_memory_space_constraint(x, pltpu.VMEM)

SMEM = pl.BlockSpec(memory_space=pltpu.SMEM)


def bf16_parts(x):
    top = x.astype(bf16)
    rest = x - top.astype(f32)
    middle = rest.astype(bf16)
    return top, middle, (rest - middle.astype(f32)).astype(bf16)


def dot(a, b, dims=((1,), (0,))):
    return lax.dot_general(a, b, (dims, ((), ())), preferred_element_type=f32)


def dot_f32(a, b, dims=((1,), (0,))):
    a0, a1, a2 = bf16_parts(a)
    b0, b1, b2 = bf16_parts(b)
    return dot(
        jnp.concatenate([a0, a0, a1, a0, a2, a1], axis=dims[0][0]),
        jnp.concatenate([b0, b1, b0, b2, b0, b1], axis=dims[1][0]),
        dims,
    )


def pack_kernel(slab, gain, diag, out):
    size = BLOCK
    out[0:size, :] = slab[0:size, :]
    rows = [*bf16_parts(gain[0:1, :]), *bf16_parts(diag[0:1, :])]
    rows.append(jnp.zeros((out.shape[0] - size - len(rows), size), bf16))
    out[size:, :] = jnp.concatenate(rows, axis=0)


def image_kernel(scale, which_ref, coef_ref, offset_ref, *refs):
    slabs, edges = refs[:4], refs[4:8]
    gain_ref, diag_ref, first, second, share, gathered, scaled, gains, diags = refs[8:]
    modes = gathered.shape[0]
    size = BLOCK
    tiles = gain_ref.shape[0]
    rows = tiles * size
    for distance in range(modes):
        m = which_ref[0] ^ distance
        gathered[m, 0:rows, :] = slabs[distance][...]
        gathered[m, rows:, :] = edges[distance][0:size, :]
    split = first.shape[0]
    wide = size + 2 * BAND
    row = lax.broadcasted_iota(jnp.int32, (size, wide), 0)
    column = lax.broadcasted_iota(jnp.int32, (size, wide), 1)
    distance = jnp.abs(column - row - BAND)
    band = jnp.zeros((size, wide), f32)
    for j in range(NOFF):
        band = band + jnp.where(distance == offset_ref[j], coef_ref[j], 0.0)
    parts = bf16_parts(band)
    across_end = jnp.logical_and(which_ref[1] != 0, (row < size - BAND) != (column < size))
    last_parts = bf16_parts(jnp.where(across_end, 0.0, band))
    tail = edges[0][size:, :].astype(f32)
    next_gain = tail[0:1, :] + tail[1:2, :] + tail[2:3, :]
    next_diag = tail[3:4, :] + tail[4:5, :] + tail[5:6, :]
    for ref, own, extra in ((gains, gain_ref, next_gain), (diags, diag_ref, next_diag)):
        filler = jnp.zeros((8 - (tiles + 1) % 8, size), f32)
        turned = jnp.transpose(jnp.concatenate([own[...], extra, filler], axis=0))
        for i in range(tiles + 1):
            ref[i * size : (i + 1) * size, :] = jnp.broadcast_to(turned[:, i : i + 1], (size, size))
    for m in range(modes):
        lanes = slice(m * size, (m + 1) * size)
        scaled[:, lanes] = (gains[...] * gathered[m].astype(f32)).astype(bf16)
    for i in range(tiles):
        rows_in = scaled[i * size : i * size + wide, :]
        p = last_parts if i == tiles - 1 else parts
        neighbour = dot(p[0], rows_in) + dot(p[1], rows_in) + dot(p[2], rows_in)
        here = slice(BAND + i * size, BAND + (i + 1) * size)
        gain, diag = gains[here, :], diags[here, :]
        for m in range(modes):
            lanes = slice(m * size, (m + 1) * size)
            value = (diag * gathered[m, here, :].astype(f32) + gain * neighbour[:, lanes]).astype(bf16)
            for image, low, high in ((first, 0, split), (second, split, rows)):
                a, b = max(low, i * size), min(high, (i + 1) * size)
                if a < b:
                    image[a - low : b - low, lanes] = value[a - i * size : b - i * size, :]

    def block(s):
        i, j = which_ref[2 + 2 * s], which_ref[3 + 2 * s]
        total = jnp.zeros((size, size), f32)
        for image, at in ((first, BAND), (second, BAND + split)):
            image_i = image[:, pl.ds(pl.multiple_of(i * size, size), size)]
            image_j = image[:, pl.ds(pl.multiple_of(j * size, size), size)]
            slab_i = gathered[i, at : at + image.shape[0], :]
            slab_j = gathered[j, at : at + image.shape[0], :]
            over_rows = ((0,), (0,))
            total = total + dot(image_i, slab_j, over_rows) + dot(slab_i, image_j, over_rows)
        return total * scale

    row = lax.broadcasted_iota(jnp.int32, (size, size), 0)
    column = lax.broadcasted_iota(jnp.int32, (size, size), 1)
    upper = block(1)
    share[0:size, :] = jnp.where(row >= column, block(0), upper)
    share[size : 2 * size, :] = block(2)
    diagonal = jnp.sum(jnp.where(row == column, upper, 0.0), axis=0, keepdims=True)
    share[2 * size :, :] = jnp.broadcast_to(diagonal, (8, size))


def lanes_of(x, t):
    return jnp.broadcast_to(x[:, t : t + 1], (8, BLOCK))


def rows_of(x, t):
    return jnp.broadcast_to(x[t : t + 1, :], (8, BLOCK))


def inverse_factor(square, beside, depth=3):
    panels = BLOCK // 8
    sub = lax.broadcasted_iota(jnp.int32, (8, BLOCK), 0)
    lane = lax.broadcasted_iota(jnp.int32, (8, BLOCK), 1)
    rows = [square[8 * p : 8 * p + 8, :] for p in range(panels)]
    own = [lanes_of(rows[0], t) for t in range(8)]
    result = []
    for p in range(panels):
        below = range(p + 1, min(panels, p + 1 + depth))
        under = {i: [lanes_of(rows[i], 8 * p + t) for t in range(8)] for i in below}
        ahead = [lanes_of(rows[p + 1], 8 * p + 8 + t) for t in range(8)] if p + 1 < panels else []
        inside = jnp.logical_and(lane >= 8 * p, lane < 8 * p + 8)
        a = jnp.where(inside, (lane == sub + 8 * p).astype(f32), rows[p])
        for i in below:
            rows[i] = jnp.where(inside, 0.0, rows[i])
        pivots = jnp.ones((8, BLOCK), f32)
        inverses = jnp.ones((8, BLOCK), f32)
        for t in range(8):
            pivot = rows_of(own[t], t)
            inverse = 1.0 / pivot
            pivots = jnp.where(sub == t, pivot, pivots)
            inverses = jnp.where(sub == t, inverse, inverses)
            f = jnp.where(sub > t, own[t], 0.0) * inverse
            g = {i: under[i][t] * inverse for i in below}
            for u in range(t + 1, 8):
                u_row = rows_of(own[u], t)
                own[u] = own[u] - f * u_row
                for i in below:
                    under[i][u] = under[i][u] - g[i] * u_row
            for u in range(len(ahead)):
                ahead[u] = ahead[u] - g[p + 1] * rows_of(under[p + 1][t], u)
            a_row = rows_of(a, t)
            if t < 7:
                a = a - f * a_row
            for i in below:
                rows[i] = rows[i] - g[i] * a_row
        result.append(jnp.where(lane < 8 * p + 8, a * lax.rsqrt(pivots), 0.0))
        own = ahead
        for _ in range(-(-len(beside) // (panels - p))):
            beside.pop(0)()
        rest = p + 1 + depth
        if rest < panels:
            a0, a1, a2 = bf16_parts(a * inverses)
            b0, b1, b2 = bf16_parts(a)
            update = dot(
                jnp.concatenate([a0, a0, a1, a0, a2, a1], axis=0)[:, 8 * rest :],
                jnp.concatenate([b0, b1, b0, b2, b0, b1], axis=0),
                ((0,), (0,)),
            )
            for i in range(rest, panels):
                at = slice(8 * (i - rest), 8 * (i - rest) + 8)
                rows[i] = jnp.where(inside, 0.0, rows[i]) - update[at, :]
    return jnp.concatenate(result, axis=0)


def factor_kernel(which_ref, share, beside, across, opposite, inverse, gram, schur, solved):
    for distance, part in enumerate((share, beside, across, opposite)):
        gram[which_ref[0] ^ distance] = part[...]
    count = inverse.shape[1] // BLOCK
    size = BLOCK
    place = lambda i, j: slice((i * (i + 1) // 2 + j) * size, (i * (i + 1) // 2 + j + 1) * size)
    across = ((1,), (1,))
    row = lax.broadcasted_iota(jnp.int32, (size, size), 0)
    column = lax.broadcasted_iota(jnp.int32, (size, size), 1)
    blocks = {}
    for m, (one, two, three) in enumerate(SHARES):
        blocks[three] = (m, size)
        if one == two:
            blocks[one] = (m, 0)

    def diagonal(m, second):
        square = gram[m, 0:size, :]
        turned = jnp.transpose(square)
        if not second:
            return jnp.where(row >= column, square, turned)
        middle = jnp.broadcast_to(gram[m, 2 * size : 2 * size + 1, :], (size, size))
        return jnp.where(row < column, square, jnp.where(row == column, middle, turned))

    def symmetric(k):
        for m, (one, two, _) in enumerate(SHARES):
            if one != two and (k, k) in (one, two):
                return diagonal(m, (k, k) == two)

    def original(i, j):
        if i == j:
            return symmetric(i)
        m, at = blocks[i, j]
        return gram[m, at : at + size, :]

    lower = {}

    def lower_block(i, k, w):
        lower[i, k] = dot_f32(current(i, k), w, across)

    def current(i, j):
        return schur[place(i, j), :] if j else original(i, j)

    def update(i, j, k):
        value = schur[place(i, j), :] if k else original(i, j)
        schur[place(i, j), :] = value - dot_f32(lower[i, k], lower[j, k], across)

    def solve(i, k):
        there, done = slice(i * size, (i + 1) * size), (k + 1) * size
        product = dot_f32(lower[i, k], solved[k * size : done, :done])
        if k:
            product = product + jnp.concatenate(
                [solved[there, : k * size], jnp.zeros((size, size), f32)], axis=1
            )
        solved[there, :done] = product

    beside = []
    for k in range(count):
        w = inverse_factor(current(k, k), beside)
        here = slice(k * size, (k + 1) * size)
        if k + 1 < count:
            lower_block(k + 1, k, w)
            update(k + 1, k + 1, k)

        def finish(k=k, w=w, here=here):
            if k:
                solved[here, : k * size] = -dot_f32(w, solved[here, : k * size])
            solved[here, here] = w
            if k + 1 < count:
                solved[here, (k + 1) * size :] = jnp.zeros((size, (count - 1 - k) * size), f32)

        beside = [finish] if k + 1 < count else []
        for i in range(k + 2, count):
            beside.append(lambda i=i, k=k, w=w: lower_block(i, k, w))
        for i in range(k + 1, count):
            beside.append(lambda i=i, k=k: solve(i, k))
        for i in range(k + 2, count):
            for j in range(k + 1, i + 1):
                beside.append(lambda i=i, j=j, k=k: update(i, j, k))
        if k + 1 == count:
            finish()
    mine = pl.multiple_of(which_ref[0] * size, size)
    inverse[...] = solved[pl.ds(mine, size), :].astype(bf16)


def project_kernel(blocks_ref, counts_ref, low, first, second, high, inverse, shapes, out, basis, picked):
    size = BLOCK
    across = ((1,), (1,))
    at = 0
    for part in (low, first, second, high):
        basis[at : at + part.shape[0], :] = dot(part[...], inverse[...], across).astype(bf16)
        at += part.shape[0]
    for c in range(out.shape[0]):
        for s in range(BMAX):
            start = pl.multiple_of(blocks_ref[BMAX * c + s] * size, size)
            rows = basis[pl.ds(start, size), :]
            picked[s * size : (s + 1) * size, :] = jnp.where(s < counts_ref[c], rows, jnp.zeros_like(rows))
        out[c] = dot(picked[...], shapes[c], ((0,), (0,))).astype(bf16)


def exchange(value, axis, step):
    return lax.ppermute(value, axis, [(i, i ^ step) for i in range(lax.axis_size(axis))])


def from_modes(value):
    across = exchange(value, "modes", 2)
    beside = exchange(value, "modes", 1)
    return value, beside, across, exchange(across, "modes", 1)


def sum_over_rows(value):
    step = lax.axis_size("rows") // 2
    while step:
        value = value + exchange(value, "rows", step)
        step //= 2
    return value


def local(
    mode_slab,
    mass_diag,
    mass_gain,
    band_coef,
    band_offsets,
    boundary_blocks,
    boundary_counts,
    boundary_modes,
):
    rows_dev, mode_cols = mode_slab.shape
    modes = lax.axis_size("modes")
    row_devices = lax.axis_size("rows")
    order = mode_cols * modes
    count = order // BLOCK
    per_dev = rows_dev // BLOCK
    rim_rows = per_dev // 2 * BLOCK
    total_rows = rows_dev * row_devices
    assert modes == len(SHARES) and order == modes * BLOCK and mode_cols == BLOCK
    assert rows_dev == 2 * rim_rows and row_devices & (row_devices - 1) == 0
    around = [(i, (i + 1) % row_devices) for i in range(row_devices)]
    back = [(target, source) for source, target in around]
    gain_rows = near(mass_gain.reshape(per_dev, BLOCK))
    diag_rows = near(mass_diag.reshape(per_dev, BLOCK))

    packed = pl.pallas_call(
        pack_kernel,
        out_shape=pltpu.VMEM((BLOCK + 16, mode_cols), bf16),
        in_specs=[VMEM, VMEM, VMEM],
        out_specs=VMEM,
        name="pack",
    )(mode_slab, mass_gain.reshape(per_dev, BLOCK), mass_diag.reshape(per_dev, BLOCK))
    edge = lax.ppermute(packed, "rows", back)
    slabs = from_modes(mode_slab)
    edges = [edge] + [exchange(edge, "modes", d) for d in (1, 2, 3)]

    mode_index = lax.axis_index("modes")
    is_last = lax.axis_index("rows") == row_devices - 1
    blocks = jnp.asarray(SHARES, jnp.int32).reshape(modes, -1)[mode_index]
    which = jnp.concatenate([jnp.stack([mode_index, is_last.astype(jnp.int32)]).astype(jnp.int32), blocks])
    extended = rows_dev + BLOCK
    first, second, share = pl.pallas_call(
        lambda *refs: image_kernel(0.5 / total_rows, *refs),
        out_shape=(
            pltpu.VMEM((rim_rows - BAND, order), bf16),
            pltpu.VMEM((rim_rows + BAND, order), bf16),
            pltpu.VMEM((2 * BLOCK + 8, BLOCK), f32),
        ),
        in_specs=[SMEM, SMEM, SMEM] + [VMEM] * 10,
        out_specs=(VMEM, VMEM, VMEM),
        scratch_shapes=[
            pltpu.VMEM((modes, extended, BLOCK), bf16),
            pltpu.VMEM((extended, order), bf16),
            pltpu.VMEM((extended, BLOCK), f32),
            pltpu.VMEM((extended, BLOCK), f32),
        ],
        name="image",
    )(which, band_coef, band_offsets, *map(near, slabs), *map(near, edges), gain_rows, diag_rows)

    share = sum_over_rows(share)
    share, one, two = lax.optimization_barrier((share, first, second))
    across = exchange(share, "modes", 2)
    beside = exchange(share, "modes", 1)
    rim_low = lax.ppermute(two, "rows", around)
    rim_high = lax.ppermute(one, "rows", back)
    opposite = exchange(across, "modes", 1)

    inverse = pl.pallas_call(
        factor_kernel,
        out_shape=pltpu.VMEM((BLOCK, order), bf16),
        in_specs=[SMEM, VMEM, VMEM, VMEM, VMEM],
        out_specs=VMEM,
        scratch_shapes=[
            pltpu.VMEM((modes, 2 * BLOCK + 8, BLOCK), f32),
            pltpu.VMEM((count * (count + 1) // 2 * BLOCK, BLOCK), f32),
            pltpu.VMEM((order, order), f32),
        ],
        name="factor",
    )(which, near(share), near(beside), near(across), near(opposite))

    total_blocks = per_dev * row_devices
    window_start = lax.axis_index("rows") * per_dev - per_dev // 2
    local_blocks = jnp.mod(boundary_blocks - window_start, total_blocks).reshape(-1)
    owned, _, width = boundary_modes.shape
    window = per_dev + 2 * (per_dev // 2)
    return pl.pallas_call(
        project_kernel,
        out_shape=jax.ShapeDtypeStruct((owned, mode_cols, width), bf16),
        in_specs=[SMEM, SMEM, VMEM, VMEM, VMEM, VMEM, VMEM, VMEM],
        out_specs=VMEM,
        scratch_shapes=[
            pltpu.VMEM((window * BLOCK, BLOCK), bf16),
            pltpu.VMEM((BMAX * BLOCK, BLOCK), bf16),
        ],
        name="project",
    )(local_blocks, boundary_counts, near(rim_low), near(first), near(second), near(rim_high), near(inverse), near(boundary_modes))


def solution(mesh):
    in_specs = (
        P("rows", "modes"),
        P("rows"),
        P("rows"),
        P(),
        P(),
        P("rows", None),
        P("rows"),
        P("rows", None, None),
    )
    out_specs = P("rows", "modes", None)
    return jax.shard_map(local, mesh=mesh, in_specs=in_specs, out_specs=out_specs, check_vma=False)
```

```python
import jax
import jax.numpy as jnp
from jax import lax
from jax.experimental import pallas as pl
from jax.experimental.pallas import tpu as pltpu
from jax.sharding import PartitionSpec as P

BLOCK = 128
BMAX = 4
NOFF = 4
BAND = 64
SHARES = (
    ((0, 0), (1, 1), (1, 0)),
    ((2, 2), (3, 3), (2, 0)),
    ((2, 1), (2, 1), (3, 0)),
    ((3, 1), (3, 1), (3, 2)),
)

f32 = jnp.float32
bf16 = jnp.bfloat16
VMEM = pl.BlockSpec(memory_space=pltpu.VMEM)


def near(x):
    return pltpu.with_memory_space_constraint(x, pltpu.VMEM)

SMEM = pl.BlockSpec(memory_space=pltpu.SMEM)


def bf16_parts(x):
    top = x.astype(bf16)
    rest = x - top.astype(f32)
    middle = rest.astype(bf16)
    return top, middle, (rest - middle.astype(f32)).astype(bf16)


def dot(a, b, dims=((1,), (0,))):
    return lax.dot_general(a, b, (dims, ((), ())), preferred_element_type=f32)


def dot_f32(a, b, dims=((1,), (0,))):
    a0, a1, a2 = bf16_parts(a)
    b0, b1, b2 = bf16_parts(b)
    return dot(
        jnp.concatenate([a0, a0, a1, a0, a2, a1], axis=dims[0][0]),
        jnp.concatenate([b0, b1, b0, b2, b0, b1], axis=dims[1][0]),
        dims,
    )


def pack_kernel(slab, gain, diag, out):
    size = BLOCK
    out[0:size, :] = slab[0:size, :]
    rows = [*bf16_parts(gain[0:1, :]), *bf16_parts(diag[0:1, :])]
    rows.append(jnp.zeros((out.shape[0] - size - len(rows), size), bf16))
    out[size:, :] = jnp.concatenate(rows, axis=0)


def image_kernel(scale, which_ref, coef_ref, offset_ref, *refs):
    slabs, edges = refs[:4], refs[4:8]
    gain_ref, diag_ref, first, second, share, gathered, scaled, gains, diags = refs[8:]
    modes = gathered.shape[0]
    size = BLOCK
    tiles = gain_ref.shape[0]
    rows = tiles * size
    for distance in range(modes):
        m = which_ref[0] ^ distance
        gathered[m, 0:rows, :] = slabs[distance][...]
        gathered[m, rows:, :] = edges[distance][0:size, :]
    split = first.shape[0]
    wide = size + 2 * BAND
    row = lax.broadcasted_iota(jnp.int32, (size, wide), 0)
    column = lax.broadcasted_iota(jnp.int32, (size, wide), 1)
    distance = jnp.abs(column - row - BAND)
    band = jnp.zeros((size, wide), f32)
    for j in range(NOFF):
        band = band + jnp.where(distance == offset_ref[j], coef_ref[j], 0.0)
    parts = bf16_parts(band)
    across_end = jnp.logical_and(which_ref[1] != 0, (row < size - BAND) != (column < size))
    last_parts = bf16_parts(jnp.where(across_end, 0.0, band))
    tail = edges[0][size:, :].astype(f32)
    next_gain = tail[0:1, :] + tail[1:2, :] + tail[2:3, :]
    next_diag = tail[3:4, :] + tail[4:5, :] + tail[5:6, :]
    for ref, own, extra in ((gains, gain_ref, next_gain), (diags, diag_ref, next_diag)):
        filler = jnp.zeros((8 - (tiles + 1) % 8, size), f32)
        turned = jnp.transpose(jnp.concatenate([own[...], extra, filler], axis=0))
        for i in range(tiles + 1):
            ref[i * size : (i + 1) * size, :] = jnp.broadcast_to(turned[:, i : i + 1], (size, size))
    for m in range(modes):
        lanes = slice(m * size, (m + 1) * size)
        scaled[:, lanes] = (gains[...] * gathered[m].astype(f32)).astype(bf16)
    for i in range(tiles):
        rows_in = scaled[i * size : i * size + wide, :]
        p = last_parts if i == tiles - 1 else parts
        neighbour = dot(p[0], rows_in) + dot(p[1], rows_in) + dot(p[2], rows_in)
        here = slice(BAND + i * size, BAND + (i + 1) * size)
        gain, diag = gains[here, :], diags[here, :]
        for m in range(modes):
            lanes = slice(m * size, (m + 1) * size)
            value = (diag * gathered[m, here, :].astype(f32) + gain * neighbour[:, lanes]).astype(bf16)
            for image, low, high in ((first, 0, split), (second, split, rows)):
                a, b = max(low, i * size), min(high, (i + 1) * size)
                if a < b:
                    image[a - low : b - low, lanes] = value[a - i * size : b - i * size, :]

    def block(s):
        i, j = which_ref[2 + 2 * s], which_ref[3 + 2 * s]
        total = jnp.zeros((size, size), f32)
        for image, at in ((first, BAND), (second, BAND + split)):
            image_i = image[:, pl.ds(pl.multiple_of(i * size, size), size)]
            image_j = image[:, pl.ds(pl.multiple_of(j * size, size), size)]
            slab_i = gathered[i, at : at + image.shape[0], :]
            slab_j = gathered[j, at : at + image.shape[0], :]
            over_rows = ((0,), (0,))
            total = total + dot(image_i, slab_j, over_rows) + dot(slab_i, image_j, over_rows)
        return total * scale

    row = lax.broadcasted_iota(jnp.int32, (size, size), 0)
    column = lax.broadcasted_iota(jnp.int32, (size, size), 1)
    upper = block(1)
    share[0:size, :] = jnp.where(row >= column, block(0), upper)
    share[size : 2 * size, :] = block(2)
    diagonal = jnp.sum(jnp.where(row == column, upper, 0.0), axis=0, keepdims=True)
    share[2 * size :, :] = jnp.broadcast_to(diagonal, (8, size))


def lanes_of(x, t):
    return jnp.broadcast_to(x[:, t : t + 1], (8, BLOCK))


def rows_of(x, t):
    return jnp.broadcast_to(x[t : t + 1, :], (8, BLOCK))


def inverse_factor(square, beside, depth=3):
    panels = BLOCK // 8
    sub = lax.broadcasted_iota(jnp.int32, (8, BLOCK), 0)
    lane = lax.broadcasted_iota(jnp.int32, (8, BLOCK), 1)
    rows = [square[8 * p : 8 * p + 8, :] for p in range(panels)]
    own = [lanes_of(rows[0], t) for t in range(8)]
    result = []
    for p in range(panels):
        has_next = p + 1 < panels
        inside = jnp.logical_and(lane >= 8 * p, lane < 8 * p + 8)
        a = jnp.where(inside, (lane == sub + 8 * p).astype(f32), rows[p])
        ahead = []
        if has_next:
            under = [lanes_of(rows[p + 1], 8 * p + t) for t in range(8)]
            ahead = [lanes_of(rows[p + 1], 8 * p + 8 + t) for t in range(8)]
            c = jnp.where(inside, 0.0, rows[p + 1])
        pivots = jnp.ones((8, BLOCK), f32)
        inverses = jnp.ones((8, BLOCK), f32)
        steps = []
        for t in range(8):
            pivot = rows_of(own[t], t)
            inverse = 1.0 / pivot
            pivots = jnp.where(sub == t, pivot, pivots)
            inverses = jnp.where(sub == t, inverse, inverses)
            f = jnp.where(sub > t, own[t], 0.0) * inverse
            a_row = rows_of(a, t)
            u_rows = {u: rows_of(own[u], t) for u in range(t + 1, 8)}
            steps.append((inverse, u_rows, a_row))
            for u in range(t + 1, 8):
                own[u] = own[u] - f * u_rows[u]
            if t < 7:
                a = a - f * a_row
            if has_next:
                g = under[t] * inverse
                for u in range(t + 1, 8):
                    under[u] = under[u] - g * u_rows[u]
                for u in range(8):
                    ahead[u] = ahead[u] - g * rows_of(under[t], u)
                c = c - g * a_row
        result.append(jnp.where(lane < 8 * p + 8, a * lax.rsqrt(pivots), 0.0))
        for i in range(p + 2, min(panels, p + 1 + depth)):
            below = [lanes_of(rows[i], 8 * p + t) for t in range(8)]
            d = jnp.where(inside, 0.0, rows[i])
            for t, (inverse, u_rows, a_row) in enumerate(steps):
                g = below[t] * inverse
                for u in range(t + 1, 8):
                    below[u] = below[u] - g * u_rows[u]
                d = d - g * a_row
            rows[i] = d
        if has_next:
            rows[p + 1] = c
        own = ahead
        for _ in range(-(-len(beside) // (panels - p))):
            beside.pop(0)()
        rest = p + 1 + depth
        if rest < panels:
            a0, a1, a2 = bf16_parts(a * inverses)
            b0, b1, b2 = bf16_parts(a)
            update = dot(
                jnp.concatenate([a0, a0, a1, a0, a2, a1], axis=0)[:, 8 * rest :],
                jnp.concatenate([b0, b1, b0, b2, b0, b1], axis=0),
                ((0,), (0,)),
            )
            for i in range(rest, panels):
                at = slice(8 * (i - rest), 8 * (i - rest) + 8)
                rows[i] = jnp.where(inside, 0.0, rows[i]) - update[at, :]
    return jnp.concatenate(result, axis=0)


def factor_kernel(which_ref, share, beside, across, opposite, inverse, gram, schur, solved):
    for distance, part in enumerate((share, beside, across, opposite)):
        gram[which_ref[0] ^ distance] = part[...]
    count = inverse.shape[1] // BLOCK
    size = BLOCK
    place = lambda i, j: slice((i * (i + 1) // 2 + j) * size, (i * (i + 1) // 2 + j + 1) * size)
    across = ((1,), (1,))
    row = lax.broadcasted_iota(jnp.int32, (size, size), 0)
    column = lax.broadcasted_iota(jnp.int32, (size, size), 1)
    blocks = {}
    for m, (one, two, three) in enumerate(SHARES):
        blocks[three] = (m, size)
        if one == two:
            blocks[one] = (m, 0)

    def diagonal(m, second):
        square = gram[m, 0:size, :]
        turned = jnp.transpose(square)
        if not second:
            return jnp.where(row >= column, square, turned)
        middle = jnp.broadcast_to(gram[m, 2 * size : 2 * size + 1, :], (size, size))
        return jnp.where(row < column, square, jnp.where(row == column, middle, turned))

    def symmetric(k):
        for m, (one, two, _) in enumerate(SHARES):
            if one != two and (k, k) in (one, two):
                return diagonal(m, (k, k) == two)

    def original(i, j):
        if i == j:
            return symmetric(i)
        m, at = blocks[i, j]
        return gram[m, at : at + size, :]

    lower = {}

    def lower_block(i, k, w):
        lower[i, k] = dot_f32(current(i, k), w, across)

    def current(i, j):
        return schur[place(i, j), :] if j else original(i, j)

    def update(i, j, k):
        value = schur[place(i, j), :] if k else original(i, j)
        schur[place(i, j), :] = value - dot_f32(lower[i, k], lower[j, k], across)

    def solve(i, k):
        there, done = slice(i * size, (i + 1) * size), (k + 1) * size
        product = dot_f32(lower[i, k], solved[k * size : done, :done])
        if k:
            product = product + jnp.concatenate(
                [solved[there, : k * size], jnp.zeros((size, size), f32)], axis=1
            )
        solved[there, :done] = product

    beside = []
    for k in range(count):
        w = inverse_factor(current(k, k), beside)
        here = slice(k * size, (k + 1) * size)
        if k + 1 < count:
            lower_block(k + 1, k, w)
            update(k + 1, k + 1, k)

        def finish(k=k, w=w, here=here):
            if k:
                solved[here, : k * size] = -dot_f32(w, solved[here, : k * size])
            solved[here, here] = w
            if k + 1 < count:
                solved[here, (k + 1) * size :] = jnp.zeros((size, (count - 1 - k) * size), f32)

        beside = [finish] if k + 1 < count else []
        for i in range(k + 2, count):
            beside.append(lambda i=i, k=k, w=w: lower_block(i, k, w))
        for i in range(k + 1, count):
            beside.append(lambda i=i, k=k: solve(i, k))
        for i in range(k + 2, count):
            for j in range(k + 1, i + 1):
                beside.append(lambda i=i, j=j, k=k: update(i, j, k))
        if k + 1 == count:
            finish()
    mine = pl.multiple_of(which_ref[0] * size, size)
    inverse[...] = solved[pl.ds(mine, size), :].astype(bf16)


def project_kernel(blocks_ref, counts_ref, low, first, second, high, inverse, shapes, out, basis, picked):
    size = BLOCK
    across = ((1,), (1,))
    at = 0
    for part in (low, first, second, high):
        basis[at : at + part.shape[0], :] = dot(part[...], inverse[...], across).astype(bf16)
        at += part.shape[0]
    for c in range(out.shape[0]):
        for s in range(BMAX):
            start = pl.multiple_of(blocks_ref[BMAX * c + s] * size, size)
            rows = basis[pl.ds(start, size), :]
            picked[s * size : (s + 1) * size, :] = jnp.where(s < counts_ref[c], rows, jnp.zeros_like(rows))
        out[c] = dot(picked[...], shapes[c], ((0,), (0,))).astype(bf16)


def exchange(value, axis, step):
    return lax.ppermute(value, axis, [(i, i ^ step) for i in range(lax.axis_size(axis))])


def from_modes(value):
    across = exchange(value, "modes", 2)
    beside = exchange(value, "modes", 1)
    return value, beside, across, exchange(across, "modes", 1)


def sum_over_rows(value):
    step = lax.axis_size("rows") // 2
    while step:
        value = value + exchange(value, "rows", step)
        step //= 2
    return value


def local(
    mode_slab,
    mass_diag,
    mass_gain,
    band_coef,
    band_offsets,
    boundary_blocks,
    boundary_counts,
    boundary_modes,
):
    rows_dev, mode_cols = mode_slab.shape
    modes = lax.axis_size("modes")
    row_devices = lax.axis_size("rows")
    order = mode_cols * modes
    count = order // BLOCK
    per_dev = rows_dev // BLOCK
    rim_rows = per_dev // 2 * BLOCK
    total_rows = rows_dev * row_devices
    assert modes == len(SHARES) and order == modes * BLOCK and mode_cols == BLOCK
    assert rows_dev == 2 * rim_rows and row_devices & (row_devices - 1) == 0
    around = [(i, (i + 1) % row_devices) for i in range(row_devices)]
    back = [(target, source) for source, target in around]
    gain_rows = near(mass_gain.reshape(per_dev, BLOCK))
    diag_rows = near(mass_diag.reshape(per_dev, BLOCK))

    packed = pl.pallas_call(
        pack_kernel,
        out_shape=pltpu.VMEM((BLOCK + 16, mode_cols), bf16),
        in_specs=[VMEM, VMEM, VMEM],
        out_specs=VMEM,
        name="pack",
    )(mode_slab, mass_gain.reshape(per_dev, BLOCK), mass_diag.reshape(per_dev, BLOCK))
    edge = lax.ppermute(packed, "rows", back)
    slabs = from_modes(mode_slab)
    edges = [edge] + [exchange(edge, "modes", d) for d in (1, 2, 3)]

    mode_index = lax.axis_index("modes")
    is_last = lax.axis_index("rows") == row_devices - 1
    blocks = jnp.asarray(SHARES, jnp.int32).reshape(modes, -1)[mode_index]
    which = jnp.concatenate([jnp.stack([mode_index, is_last.astype(jnp.int32)]).astype(jnp.int32), blocks])
    extended = rows_dev + BLOCK
    first, second, share = pl.pallas_call(
        lambda *refs: image_kernel(0.5 / total_rows, *refs),
        out_shape=(
            pltpu.VMEM((rim_rows - BAND, order), bf16),
            pltpu.VMEM((rim_rows + BAND, order), bf16),
            pltpu.VMEM((2 * BLOCK + 8, BLOCK), f32),
        ),
        in_specs=[SMEM, SMEM, SMEM] + [VMEM] * 10,
        out_specs=(VMEM, VMEM, VMEM),
        scratch_shapes=[
            pltpu.VMEM((modes, extended, BLOCK), bf16),
            pltpu.VMEM((extended, order), bf16),
            pltpu.VMEM((extended, BLOCK), f32),
            pltpu.VMEM((extended, BLOCK), f32),
        ],
        name="image",
    )(which, band_coef, band_offsets, *map(near, slabs), *map(near, edges), gain_rows, diag_rows)

    share = sum_over_rows(share)
    share, one, two = lax.optimization_barrier((share, first, second))
    across = exchange(share, "modes", 2)
    beside = exchange(share, "modes", 1)
    rim_low = lax.ppermute(two, "rows", around)
    rim_high = lax.ppermute(one, "rows", back)
    opposite = exchange(across, "modes", 1)

    inverse = pl.pallas_call(
        factor_kernel,
        out_shape=pltpu.VMEM((BLOCK, order), bf16),
        in_specs=[SMEM, VMEM, VMEM, VMEM, VMEM],
        out_specs=VMEM,
        scratch_shapes=[
            pltpu.VMEM((modes, 2 * BLOCK + 8, BLOCK), f32),
            pltpu.VMEM((count * (count + 1) // 2 * BLOCK, BLOCK), f32),
            pltpu.VMEM((order, order), f32),
        ],
        name="factor",
    )(which, near(share), near(beside), near(across), near(opposite))

    total_blocks = per_dev * row_devices
    window_start = lax.axis_index("rows") * per_dev - per_dev // 2
    local_blocks = jnp.mod(boundary_blocks - window_start, total_blocks).reshape(-1)
    owned, _, width = boundary_modes.shape
    window = per_dev + 2 * (per_dev // 2)
    return pl.pallas_call(
        project_kernel,
        out_shape=jax.ShapeDtypeStruct((owned, mode_cols, width), bf16),
        in_specs=[SMEM, SMEM, VMEM, VMEM, VMEM, VMEM, VMEM, VMEM],
        out_specs=VMEM,
        scratch_shapes=[
            pltpu.VMEM((window * BLOCK, BLOCK), bf16),
            pltpu.VMEM((BMAX * BLOCK, BLOCK), bf16),
        ],
        name="project",
    )(local_blocks, boundary_counts, near(rim_low), near(first), near(second), near(rim_high), near(inverse), near(boundary_modes))


def solution(mesh):
    in_specs = (
        P("rows", "modes"),
        P("rows"),
        P("rows"),
        P(),
        P(),
        P("rows", None),
        P("rows"),
        P("rows", None, None),
    )
    out_specs = P("rows", "modes", None)
    return jax.shard_map(local, mesh=mesh, in_specs=in_specs, out_specs=out_specs, check_vma=False)
```
